512 devices in a mesh: gy: 64 (over z, y_hi, core), ch: 8 (over y_lo, x).
Axes of the slice: x: 4, y: 4 (y_hi: 2, y_lo: 2; y = y_hi * 2 + y_lo), z: 16, core: 2. Of those that a mesh axis runs over, the one named last changes fastest.
Arguments:
- volume: bfloat16 [256, 512, 4, 128], P('ch', 'gy'), may hold values from -6 to 6
- first_weight: bfloat16 [3, 3, 3, 256, 256], P(None, None, None, 'ch'), may hold values from -0.078125 to 0.078125
- first_bias: float32 [256], P('ch'), may hold values from -3 to 3
- second_weight: bfloat16 [3, 3, 3, 256, 256], P(None, None, None, 'ch'), may hold values from -0.078125 to 0.078125
- second_bias: float32 [256], P('ch'), may hold values from -3 to 3
Outputs:
- block_out: bfloat16 [256, 512, 4, 128], P('ch', 'gy')
The draws below stay inside these ranges and needn't reach their ends.
All inputs are finite; a program needn't handle non-finite values.
Results may differ from the reference program's by a relative error of at most 0.003.
Values may be sent and summed in bfloat16 or wider, within the bound.
No kernel may reach another device: no remote copies, remote signals or barrier semaphores. Data moves between devices by JAX's collectives and lax.ppermute only.
A program may use at most 64 MiB of HBM per device.

```python
import jax
import jax.numpy as jnp
from jax import lax

C = 256
NZ = 4
NX = 128
NY = 512


def shard_levels(stream_key, extent, pieces, smallest, top_value):
    level, own = 1.0, jax.random.fold_in(stream_key, 6)
    for position, shards_of in pieces:
        draws = jnp.exp(jax.random.uniform(jax.random.fold_in(own, position), (shards_of,), jnp.float32, smallest / len(pieces), top_value / len(pieces)))
        level = level * jnp.repeat(draws, extent[position] // shards_of).reshape([-1 if axis == position else 1 for axis in range(len(extent))])
    return level


def normal_values(key, extent, width, reach, pieces=(), held_as=jnp.bfloat16):
    loudness = shard_levels(key, extent, pieces, -0.22, 0.18) if pieces else 1.0
    drawn = jax.random.normal(key, extent, jnp.float32) * width * loudness
    return jnp.minimum(jnp.maximum(drawn, -reach), reach).astype(held_as)


def setup_inputs(seed: int = 0) -> dict:
    arg_keys = jax.random.split(jax.random.key(seed), 6)
    volume = normal_values(arg_keys[0], (C, NY, NZ, NX), 1.0, 6.0, ((0, 8), (1, 64)))
    first_weight = normal_values(arg_keys[1], (3, 3, 3, C, C), (27 * C) ** -0.5, 0.078125, ((3, 8),))
    first_bias = normal_values(arg_keys[2], (C,), 0.5, 3.0, ((0, 8),), jnp.float32)
    second_weight = normal_values(arg_keys[3], (3, 3, 3, C, C), (27 * C) ** -0.5, 0.078125, ((3, 8),))
    second_bias = normal_values(arg_keys[4], (C,), 0.5, 3.0, ((0, 8),), jnp.float32)
    return dict(volume=volume, first_weight=first_weight, first_bias=first_bias, second_weight=second_weight, second_bias=second_bias)


def convolve(field, weights):
    inputs = field.astype(jnp.float32)[None]
    kernel = jnp.transpose(weights.astype(jnp.float32), (3, 4, 0, 1, 2))
    result = lax.conv_general_dilated(inputs, kernel, (1, 1, 1), ((1, 1), (1, 1), (1, 1)), dimension_numbers=("NCDHW", "OIDHW", "NCDHW"), precision=lax.Precision.HIGHEST)
    return result[0]


def reference(volume, first_weight, first_bias, second_weight, second_bias):
    before = convolve(volume, first_weight) + first_bias.astype(jnp.float32)[:, None, None, None]
    hidden = jax.nn.gelu(before, approximate=False).astype(jnp.bfloat16)
    after = convolve(hidden, second_weight) + second_bias.astype(jnp.float32)[:, None, None, None]
    return (volume.astype(jnp.float32) + after).astype(jnp.bfloat16)
```

```python
import jax
import jax.numpy as jnp
import numpy as np
from jax import lax
from jax.experimental import pallas as pl
from jax.experimental.pallas import tpu as pltpu
from jax.sharding import PartitionSpec as P

ROOT_HALF = np.float32(np.sqrt(0.5))
F32, BF16 = jnp.float32, jnp.bfloat16


def column(row_ref, n):
    i = lax.broadcasted_iota(jnp.int32, (n, n), 0)
    j = lax.broadcasted_iota(jnp.int32, (n, n), 1)
    square = jnp.where(i == j, jnp.broadcast_to(row_ref[...], (n, n)), 0.0)
    return jnp.sum(square, axis=1, keepdims=True)


def gelu(v):
    return 0.5 * v * (1.0 + lax.erf(v * ROOT_HALF))


def x_taps(a, co, nx):
    lane = lax.broadcasted_iota(jnp.int32, (co, nx), 1)
    left = jnp.where(lane == 0, 0.0, pltpu.roll(a[:co], 1, 1))
    right = jnp.where(lane == nx - 1, 0.0, pltpu.roll(a[2 * co :], nx - 1, 1))
    return a[co : 2 * co] + left + right


def z_taps(parts, co):
    nz = len(parts)
    sums = [None] * nz
    for zz in range(nz):
        for dz in range(3):
            z = zz - dz + 1
            if 0 <= z < nz:
                e = parts[zz][dz * 3 * co : (dz + 1) * 3 * co]
                sums[z] = e if sums[z] is None else sums[z] + e
    return sums


def rows(w_ref, dy):
    return w_ref[dy].reshape(-1, w_ref.shape[-1])


def cells(planes, p, z):
    n, ny, _, c, nx = planes.shape
    if not 0 <= p < ny:
        return jnp.zeros((n * c, nx), BF16)
    return planes[:, p, z].reshape(n * c, nx)


def edge_kernel(planes, w_ref, below, above):
    _, ny, nz, co, nx = planes.shape
    for out, p, dy in ((below, 0, 2), (above, ny - 1, 0)):
        parts = [
            jnp.dot(rows(w_ref, dy), cells(planes, p, zz), preferred_element_type=F32)
            for zz in range(nz)
        ]
        for z, s in enumerate(z_taps(parts, co)):
            out[z] = x_taps(s, co, nx)


def conv(planes, w_ref, bias, take):
    _, ny, nz, co, nx = planes.shape
    half = ny // 2
    for q in range(half):
        parts = []
        for zz in range(nz):
            part = None
            for dy in range(3):
                p = q + dy - 1
                x = jnp.concatenate([cells(planes, p, zz), cells(planes, p + half, zz)], axis=1)
                d = jnp.dot(rows(w_ref, dy), x, preferred_element_type=F32)
                part = d if part is None else part + d
            parts.append(part)
        sums = z_taps(parts, co)
        for h in range(2):
            take(q + h * half, [x_taps(s[:, h * nx : (h + 1) * nx], co, nx) + bias for s in sums])


def first_kernel(planes, w_ref, b_ref, out, ends, hidden, sems):
    n, ny, nz, co, nx = planes.shape
    bias = jnp.broadcast_to(column(b_ref, co), (co, nx))

    def take(y, values):
        for z, v in enumerate(values):
            if y == 0 or y == ny - 1:
                ends[y // (ny - 1), z] = v
            else:
                hidden[y - 1, z] = gelu(v).astype(BF16)

    conv(planes, w_ref, bias, take)
    copies = [
        pltpu.make_async_copy(hidden, out.at[d, 1 : ny - 1], sems.at[d]) for d in range(n)
    ]
    for c in copies:
        c.start()
    for c in copies:
        c.wait()


def first_ends_kernel(ends, below, above, _, out, hidden, sems):
    n, ny = out.shape[:2]
    copies = []
    for side, other in enumerate((below, above)):
        hidden[side] = gelu(ends[side] + other[...]).astype(BF16)
        for d in range(n):
            c = pltpu.make_async_copy(
                hidden.at[side], out.at[d, side * (ny - 1)], sems.at[side, d]
            )
            c.start()
            copies.append(c)
    for c in copies:
        c.wait()


def channels_first(values):
    return jnp.stack(values, axis=1).astype(BF16)


def second_kernel(planes, w_ref, b_ref, v_ref, out, ends, inner, sem):
    _, ny, nz, co, nx = planes.shape
    bias = jnp.broadcast_to(column(b_ref, co), (co, nx))

    def take(y, values):
        values = [v_ref[y, z].astype(F32) + v for z, v in enumerate(values)]
        if y == 0 or y == ny - 1:
            for z, v in enumerate(values):
                ends[y // (ny - 1), z] = v
        else:
            inner[:, y - 1] = channels_first(values)

    conv(planes, w_ref, bias, take)
    copy = pltpu.make_async_copy(inner, out.at[:, 1 : ny - 1], sem)
    copy.start()
    copy.wait()


def second_ends_kernel(ends, below, above, _, out, outer, sems):
    ny = out.shape[1]
    copies = []
    for side, other in enumerate((below, above)):
        outer[side] = channels_first([ends[side, z] + other[z] for z in range(ends.shape[1])])
        c = pltpu.make_async_copy(outer.at[side], out.at[:, side * (ny - 1)], sems.at[side])
        c.start()
        copies.append(c)
    for c in copies:
        c.wait()


ANY = pl.BlockSpec(memory_space=pl.ANY)
VMEM = pl.BlockSpec(memory_space=pltpu.VMEM)
DMA = pltpu.SemaphoreType.DMA
PARAMS = pltpu.CompilerParams(vmem_limit_bytes=48 << 20)


def per_device(volume, first_weight, first_bias, second_weight, second_bias):
    co, ny, nz, nx = volume.shape
    n, length = lax.axis_size("ch"), lax.axis_size("gy")
    up = [(i, i + 1) for i in range(length - 1)]
    down = [(i + 1, i) for i in range(length - 1)]
    plane = jax.ShapeDtypeStruct((nz, co, nx), F32)
    ends_type = jax.ShapeDtypeStruct((2, nz, co, nx), F32)

    def call(kernel, out_shape, in_specs, out_specs, scratch, **extra):
        return pl.pallas_call(
            kernel,
            out_shape=out_shape,
            in_specs=in_specs,
            out_specs=out_specs,
            scratch_shapes=scratch,
            compiler_params=PARAMS,
            name=kernel.__name__,
            **extra,
        )

    def edges(planes, weight):
        below, above = call(edge_kernel, (plane, plane), [VMEM, VMEM], (VMEM, VMEM), [])(planes, weight)
        return lax.ppermute(above, "gy", up), lax.ppermute(below, "gy", down)

    cells_first = jnp.transpose(volume, (1, 2, 0, 3))
    sent = jnp.broadcast_to(cells_first, (n, ny, nz, co, nx))
    main = lax.all_to_all(sent, "ch", 0, 0, tiled=True)
    lower, upper = edges(main, first_weight)
    all_hidden = jax.ShapeDtypeStruct((n, ny, nz, co, nx), BF16)
    hidden, ends = call(
        first_kernel,
        (all_hidden, ends_type),
        [VMEM, VMEM, VMEM],
        (ANY, VMEM),
        [pltpu.VMEM((ny - 2, nz, co, nx), BF16), DMA((n,))],
    )(main, first_weight, first_bias[None])
    hidden = call(
        first_ends_kernel,
        all_hidden,
        [VMEM, VMEM, VMEM, ANY],
        ANY,
        [pltpu.VMEM((2, nz, co, nx), BF16), DMA((2, n))],
        input_output_aliases={3: 0},
    )(ends, lower, upper, hidden)

    gathered = lax.all_to_all(hidden, "ch", 0, 0, tiled=True)
    lower, upper = edges(gathered, second_weight)
    out_type = jax.ShapeDtypeStruct(volume.shape, BF16)
    out, ends = call(
        second_kernel,
        (out_type, ends_type),
        [VMEM, VMEM, VMEM, VMEM],
        (ANY, VMEM),
        [pltpu.VMEM((co, ny - 2, nz, nx), BF16), DMA],
    )(gathered, second_weight, second_bias[None], cells_first)
    return call(
        second_ends_kernel,
        out_type,
        [VMEM, VMEM, VMEM, ANY],
        ANY,
        [pltpu.VMEM((2, co, nz, nx), BF16), DMA((2,))],
        input_output_aliases={3: 0},
    )(ends, lower, upper, out)


def solution(mesh):
    in_specs = (
        P("ch", "gy", None, None),
        P(None, None, None, "ch", None),
        P("ch"),
        P(None, None, None, "ch", None),
        P("ch"),
    )
    out_specs = P("ch", "gy", None, None)
    return jax.shard_map(
        per_device, mesh=mesh, in_specs=in_specs, out_specs=out_specs, check_vma=False
    )
```

```python
import jax
import jax.numpy as jnp
import numpy as np
from jax import lax
from jax.experimental import pallas as pl
from jax.experimental.pallas import tpu as pltpu
from jax.sharding import PartitionSpec as P

ROOT_HALF = np.float32(np.sqrt(0.5))
F32, BF16 = jnp.float32, jnp.bfloat16


def column(row_ref, n):
    i = lax.broadcasted_iota(jnp.int32, (n, n), 0)
    j = lax.broadcasted_iota(jnp.int32, (n, n), 1)
    square = jnp.where(i == j, jnp.broadcast_to(row_ref[...], (n, n)), 0.0)
    return jnp.sum(square, axis=1, keepdims=True)


def gelu(v):
    return 0.5 * v * (1.0 + lax.erf(v * ROOT_HALF))


def x_taps(a, co, nx):
    lane = lax.broadcasted_iota(jnp.int32, (co, nx), 1)
    left = jnp.where(lane == 0, 0.0, pltpu.roll(a[:co], 1, 1))
    right = jnp.where(lane == nx - 1, 0.0, pltpu.roll(a[2 * co :], nx - 1, 1))
    return a[co : 2 * co] + left + right


def z_taps(parts, co):
    nz = len(parts)
    sums = [None] * nz
    for zz in range(nz):
        for dz in range(3):
            z = zz - dz + 1
            if 0 <= z < nz:
                e = parts[zz][dz * 3 * co : (dz + 1) * 3 * co]
                sums[z] = e if sums[z] is None else sums[z] + e
    return sums


def rows(w_ref, dy):
    k = w_ref.shape[-1]
    if len(w_ref.shape) == 5:
        return w_ref[dy].reshape(-1, k)
    return w_ref[pl.ds(9 * dy, 9)].reshape(-1, k)


def cells(planes, p, z):
    lead, nx = planes.shape[:-4], planes.shape[-1]
    if len(lead) == 1:
        return planes[:, p, z].reshape(-1, nx)
    return jnp.concatenate([planes[:, a, p, z].reshape(-1, nx) for a in range(lead[1])], axis=0)


def edge(planes, w_ref, p, dy):
    nz, co, nx = planes.shape[-3:]
    parts = [
        jnp.dot(rows(w_ref, dy), cells(planes, p, zz), preferred_element_type=F32)
        for zz in range(nz)
    ]
    return [x_taps(s, co, nx) for s in z_taps(parts, co)]


def conv(planes, weights, take):
    ny, nz, co, nx = planes.shape[-4:]
    half = ny // 2
    none = jnp.zeros((weights[0].shape[-1], nx), BF16)
    for q in range(half):
        parts = [[] for _ in weights]
        for zz in range(nz):
            tiles = []
            for dy in range(3):
                pair = [q + dy - 1, q + dy - 1 + half]
                pair = [cells(planes, p, zz) if 0 <= p < ny else none for p in pair]
                tiles.append(jnp.concatenate(pair, axis=1))
            for j, w_ref in enumerate(weights):
                part = None
                for dy in range(3):
                    d = jnp.dot(rows(w_ref, dy), tiles[dy], preferred_element_type=F32)
                    part = d if part is None else part + d
                parts[j].append(part)
        for j in range(len(weights)):
            sums = z_taps(parts[j], co)
            for h in range(2):
                values = [x_taps(s[:, h * nx : (h + 1) * nx], co, nx) for s in sums]
                take(j, q + h * half, values)


def parcel_bias(slab, at):
    parts = slab[:, at : at + 3].astype(F32)
    return parts[:, 0:1] + parts[:, 1:2] + parts[:, 2:3]


def first_edge_kernel(planes, own, other, below, above):
    ny = planes.shape[-4]
    for out, p, dy in ((below, 0, 2), (above, ny - 1, 0)):
        for j, w_ref in enumerate((own, other)):
            for z, v in enumerate(edge(planes, w_ref, p, dy)):
                out[j, z] = v


def first_kernel(me, planes, own, other, b_ref, out, ends, other_bias, hidden, sems):
    ny, nz, co, nx = planes.shape[-4:]
    n = out.shape[0]
    slab = other[27]
    biases = [column(b_ref, co), parcel_bias(slab, 0)]
    biases = [jnp.broadcast_to(b, (co, nx)) for b in biases]
    other_bias[...] = jnp.broadcast_to(parcel_bias(slab, 3), (co, nx))

    def take(j, y, values):
        for z, v in enumerate(values):
            v = v + biases[j]
            if y == 0 or y == ny - 1:
                ends[y // (ny - 1), j, z] = v
            else:
                hidden[j, y - 1, z] = gelu(v).astype(BF16)

    conv(planes, (own, other), take)
    half = me[0] // n
    copies = []
    for j, slot in enumerate((half, 1 - half)):
        for d in range(n):
            c = pltpu.make_async_copy(hidden.at[j], out.at[d, slot, 1 : ny - 1], sems.at[j, d])
            c.start()
            copies.append(c)
    for c in copies:
        c.wait()


def first_ends_kernel(me, ends, below, above, _, out, hidden, sems):
    n, _, ny = out.shape[:3]
    half = me[0] // n
    copies = []
    for side, other in enumerate((below, above)):
        for j, slot in enumerate((half, 1 - half)):
            hidden[side, j] = gelu(ends[side, j] + other[1 - j]).astype(BF16)
            for d in range(n):
                c = pltpu.make_async_copy(
                    hidden.at[side, j], out.at[d, slot, side * (ny - 1)], sems.at[side, j, d]
                )
                c.start()
                copies.append(c)
    for c in copies:
        c.wait()


def second_edge_kernel(me, planes, own, other, outer_own, outer_other, inner_own, inner_other):
    ny = planes.shape[-4]
    half = me[0] // planes.shape[0]
    outer, inner = ((ny - 1) * half, 2 - 2 * half), ((ny - 1) * (1 - half), 2 * half)
    for at, outs in ((outer, (outer_own, outer_other)), (inner, (inner_own, inner_other))):
        for w_ref, out in zip((own, other), outs):
            for z, v in enumerate(edge(planes, w_ref, *at)):
                out[z] = v


def channels_first(values):
    return jnp.stack(values, axis=1).astype(BF16)


def two_parts(v):
    high = v.astype(BF16)
    return high, (v - high.astype(F32)).astype(BF16)


def second_kernel(me, planes, own, other, b_ref, other_bias, v_ref, inner_other, out, ends, sent, mine, sem):
    ny, nz, co, nx = planes.shape[-4:]
    n = planes.shape[0]
    half = me[0] // n
    own_bias = jnp.broadcast_to(column(b_ref, co), (co, nx))
    partner = me[0] + n - 2 * n * half

    def send(at, z, v):
        high, low = two_parts(v)
        sent[at, z] = high
        sent[at + 1, z] = low

    def take(j, y, values):
        side = y // (ny - 1)
        is_end = y == 0 or y == ny - 1
        role = half if side == 0 else 1 - half
        if j == 0:
            values = [v_ref[me[0], y, z].astype(F32) + (v + own_bias) for z, v in enumerate(values)]
            if not is_end:
                mine[:, y - 1] = channels_first(values)
                return
            for z, v in enumerate(values):
                ends[role, z] = v
            return
        values = [v_ref[partner, y, z].astype(F32) + (v + other_bias[...]) for z, v in enumerate(values)]
        for z, v in enumerate(values):
            if is_end:
                send(2 + 2 * role, z, v)
            else:
                sent[y - 1, z] = v.astype(BF16)

    conv(planes, (own, other), take)
    for z in range(nz):
        send(6, z, inner_other[z])
    copy = pltpu.make_async_copy(mine, out.at[:, pl.ds(half * ny + 1, ny - 2)], sem)
    copy.start()
    copy.wait()


def last_kernel(me, ends, inner_own, straight, across, received, _, out, whole, rest, sems):
    nz = ends.shape[1]
    ny = out.shape[1] // 2
    half = me[0] // 4
    mine, theirs = half * ny, (1 - half) * ny
    outer, inner = (ny - 1) * half, (ny - 1) * (1 - half)

    def got(at, z):
        return received[at, z].astype(F32) + received[at + 1, z].astype(F32)

    ends_at = (
        (mine + outer, lambda z: ends[0, z] + across[z]),
        (mine + inner, lambda z: ends[1, z] + got(6, z)),
        (theirs + inner, lambda z: got(2, z) + straight[z]),
        (theirs + outer, lambda z: got(4, z) + inner_own[z]),
    )
    copies = []
    for i, (at, value) in enumerate(ends_at):
        rest[i] = channels_first([value(z) for z in range(nz)])
        copies.append(pltpu.make_async_copy(rest.at[i], out.at[:, at], sems.at[i]))
        copies[-1].start()
    for y in range(ny - 2):
        whole[:, y] = channels_first([received[y, z].astype(F32) for z in range(nz)])
    copies.append(pltpu.make_async_copy(whole, out.at[:, pl.ds(theirs + 1, ny - 2)], sems.at[4]))
    copies[-1].start()
    for c in copies:
        c.wait()


ANY = pl.BlockSpec(memory_space=pl.ANY)
VMEM = pl.BlockSpec(memory_space=pltpu.VMEM)
SMEM = pl.BlockSpec(memory_space=pltpu.SMEM)
DMA = pltpu.SemaphoreType.DMA
PARAMS = pltpu.CompilerParams(vmem_limit_bytes=48 << 20)


def call(kernel, out_shape, in_specs, out_specs, scratch, **extra):
    return pl.pallas_call(
        kernel,
        out_shape=out_shape,
        in_specs=in_specs,
        out_specs=out_specs,
        scratch_shapes=scratch,
        compiler_params=PARAMS,
        name=kernel.__name__,
        **extra,
    )


def three_parts(v):
    parts = []
    for _ in range(3):
        high = lax.reduce_precision(v, 8, 7)
        parts.append(high.astype(BF16))
        v = v - high
    return parts


def per_device(volume, first_weight, first_bias, second_weight, second_bias):
    co, full, nz, nx = volume.shape
    n, length = lax.axis_size("ch"), lax.axis_size("gy")
    g, ny = n // 2, full // 2
    axes = ("gy", "ch")
    f32 = lambda *lead: jax.ShapeDtypeStruct((*lead, nz, co, nx), F32)
    bf16 = lambda *lead: jax.ShapeDtypeStruct((*lead, nz, co, nx), BF16)

    def device(row, half, x):
        return row * n + half * g + x

    def route(*moves):
        return [
            (device(row, half, x), device(row + on, there, x))
            for half, on, there in moves
            for row in range(length)
            if 0 <= row + on < length
            for x in range(g)
        ]

    to_next = route((0, 0, 1), (1, 1, 0))
    to_previous = route((1, 0, 0), (0, -1, 1))
    to_outer = route((0, -1, 0), (1, 1, 1))
    to_across = route((0, -1, 1), (1, 1, 0))
    to_partner = route((0, 0, 1), (1, 0, 0))
    weights_route = [
        (device(row ^ 2, 1 - half, x), device(row, half, x))
        for row in range(length)
        for half in range(2)
        for x in range(g)
    ]

    me = lax.axis_index("ch").astype(jnp.int32)[None]
    columns = jnp.stack(three_parts(first_bias) + three_parts(second_bias), axis=1)
    slab = jnp.pad(columns, ((0, 0), (0, first_weight.shape[4] - 6)))
    parcel = jnp.concatenate([first_weight.reshape(27, co, -1), slab[None]], axis=0)
    other_first = lax.ppermute(parcel, axes, weights_route)
    other_second = lax.ppermute(second_weight, axes, weights_route)

    cells_first = jnp.transpose(volume, (1, 2, 0, 3))
    sent = jnp.broadcast_to(cells_first.reshape(2, 1, ny, nz, co, nx), (2, g, ny, nz, co, nx))
    main = lax.all_to_all(sent.reshape(n, ny, nz, co, nx), "ch", 0, 0, tiled=True)

    below, above = call(first_edge_kernel, (f32(2), f32(2)), [VMEM] * 3, (VMEM, VMEM), [])(
        main, first_weight, other_first
    )
    lower = lax.ppermute(above, axes, to_next)
    upper = lax.ppermute(below, axes, to_previous)
    hidden, ends, other_bias = call(
        first_kernel,
        (bf16(g, 2, ny), f32(2, 2), jax.ShapeDtypeStruct((co, nx), F32)),
        [SMEM] + [VMEM] * 4,
        (ANY, VMEM, VMEM),
        [pltpu.VMEM((2, ny - 2, nz, co, nx), BF16), DMA((2, g))],
    )(me, main, first_weight, other_first, first_bias[None])
    hidden = call(
        first_ends_kernel,
        bf16(g, 2, ny),
        [SMEM] + [VMEM] * 3 + [ANY],
        ANY,
        [pltpu.VMEM((2, 2, nz, co, nx), BF16), DMA((2, 2, g))],
        input_output_aliases={4: 0},
    )(me, ends, lower, upper, hidden)

    groups = [list(range(g)), list(range(g, n))]
    gathered = lax.all_to_all(hidden, "ch", 0, 0, tiled=True, axis_index_groups=groups)

    outer_own, outer_other, inner_own, inner_other = call(
        second_edge_kernel, (f32(),) * 4, [SMEM] + [VMEM] * 3, (VMEM,) * 4, []
    )(me, gathered, second_weight, other_second)
    straight = lax.ppermute(outer_own, axes, to_outer)
    across = lax.ppermute(outer_other, axes, to_across)
    out_type = jax.ShapeDtypeStruct(volume.shape, BF16)
    out, ends, sent = call(
        second_kernel,
        (out_type, f32(2), bf16(8)),
        [SMEM] + [VMEM] * 7,
        (ANY, VMEM, VMEM),
        [pltpu.VMEM((co, ny - 2, nz, nx), BF16), DMA],
    )(me, gathered, second_weight, other_second, second_bias[None], other_bias, main, inner_other)
    received = lax.ppermute(sent, axes, to_partner)
    return call(
        last_kernel,
        out_type,
        [SMEM] + [VMEM] * 5 + [ANY],
        ANY,
        [pltpu.VMEM((co, ny - 2, nz, nx), BF16), pltpu.VMEM((4, co, nz, nx), BF16), DMA((5,))],
        input_output_aliases={6: 0},
    )(me, ends, inner_own, straight, across, received, out)


def solution(mesh):
    in_specs = (
        P("ch", "gy", None, None),
        P(None, None, None, "ch", None),
        P("ch"),
        P(None, None, None, "ch", None),
        P("ch"),
    )
    out_specs = P("ch", "gy", None, None)
    return jax.shard_map(
        per_device, mesh=mesh, in_specs=in_specs, out_specs=out_specs, check_vma=False
    )
```

```python
import jax
import jax.numpy as jnp
import numpy as np
from jax import lax
from jax.experimental import pallas as pl
from jax.experimental.pallas import tpu as pltpu
from jax.sharding import PartitionSpec as P

ROOT_HALF = np.float32(np.sqrt(0.5))
F32, BF16 = jnp.float32, jnp.bfloat16


def column(row_ref, n):
    i = lax.broadcasted_iota(jnp.int32, (n, n), 0)
    j = lax.broadcasted_iota(jnp.int32, (n, n), 1)
    square = jnp.where(i == j, jnp.broadcast_to(row_ref[...], (n, n)), 0.0)
    return jnp.sum(square, axis=1, keepdims=True)


def gelu(v):
    return 0.5 * v * (1.0 + lax.erf(v * ROOT_HALF))


def x_taps(a, co, nx):
    lane = lax.broadcasted_iota(jnp.int32, (co, nx), 1)
    left = jnp.where(lane == 0, 0.0, pltpu.roll(a[:co], 1, 1))
    right = jnp.where(lane == nx - 1, 0.0, pltpu.roll(a[2 * co :], nx - 1, 1))
    return a[co : 2 * co] + left + right


def z_taps(parts, co):
    nz = len(parts)
    sums = [None] * nz
    for zz in range(nz):
        for dz in range(3):
            z = zz - dz + 1
            if 0 <= z < nz:
                e = parts[zz][dz * 3 * co : (dz + 1) * 3 * co]
                sums[z] = e if sums[z] is None else sums[z] + e
    return sums


def rows(w_ref, dy):
    k = w_ref.shape[-1]
    if len(w_ref.shape) == 5:
        return w_ref[dy].reshape(-1, k)
    return w_ref[pl.ds(9 * dy, 9)].reshape(-1, k)


def cells(planes, p, z):
    lead, nx = planes.shape[:-4], planes.shape[-1]
    if len(lead) == 1:
        return planes[:, p, z].reshape(-1, nx)
    return jnp.concatenate([planes[:, a, p, z].reshape(-1, nx) for a in range(lead[1])], axis=0)


def edge(planes, w_ref, p, dy):
    nz, co, nx = planes.shape[-3:]
    parts = [
        jnp.dot(rows(w_ref, dy), cells(planes, p, zz), preferred_element_type=F32)
        for zz in range(nz)
    ]
    return [x_taps(s, co, nx) for s in z_taps(parts, co)]


def conv(planes, weights, take):
    ny, nz, co, nx = planes.shape[-4:]
    half = ny // 2
    none = jnp.zeros((weights[0].shape[-1], nx), BF16)
    for q in range(half):
        parts = [[] for _ in weights]
        for zz in range(nz):
            tiles = []
            for dy in range(3):
                pair = [q + dy - 1, q + dy - 1 + half]
                pair = [cells(planes, p, zz) if 0 <= p < ny else none for p in pair]
                tiles.append(jnp.concatenate(pair, axis=1))
            for j, w_ref in enumerate(weights):
                part = None
                for dy in range(3):
                    d = jnp.dot(rows(w_ref, dy), tiles[dy], preferred_element_type=F32)
                    part = d if part is None else part + d
                parts[j].append(part)
        for j in range(len(weights)):
            sums = z_taps(parts[j], co)
            for h in range(2):
                values = [x_taps(s[:, h * nx : (h + 1) * nx], co, nx) for s in sums]
                take(j, q + h * half, values)


def parcel_bias(slab, at):
    parts = slab[:, at : at + 3].astype(F32)
    return parts[:, 0:1] + parts[:, 1:2] + parts[:, 2:3]


def half_index():
    return lax.axis_index("ch") // (lax.axis_size("ch") // 2)


def spread_kernel(planes, out, sems):
    n, ny = out.shape[:2]
    copies = [
        pltpu.make_async_copy(planes.at[pl.ds(d // (n // 2) * ny, ny)], out.at[d], sems.at[d])
        for d in range(n)
    ]
    for c in copies:
        c.start()
    for c in copies:
        c.wait()


def first_edge_kernel(planes, own, fetched, swapped, below, above, other):
    ny = planes.shape[-4]
    part = fetched.shape[0]
    second = other.shape[0] - part
    core = lax.axis_index("gy") % 2
    other[pl.ds(second * core, part)] = fetched[...]
    other[pl.ds(second * (1 - core), part)] = swapped[...]
    for out, p, dy in ((below, 0, 2), (above, ny - 1, 0)):
        for j, w_ref in enumerate((own, other)):
            for z, v in enumerate(edge(planes, w_ref, p, dy)):
                out[j, z] = v


def first_kernel(planes, own, other, parcel, b_ref, out, ends, other_bias, hidden, sems):
    ny, nz, co, nx = planes.shape[-4:]
    n = out.shape[0]
    slab = parcel[parcel.shape[0] - 1]
    biases = [column(b_ref, co), parcel_bias(slab, 0)]
    biases = [jnp.broadcast_to(b, (co, nx)) for b in biases]
    other_bias[...] = jnp.broadcast_to(parcel_bias(slab, 3), (co, nx))

    def take(j, y, values):
        for z, v in enumerate(values):
            v = v + biases[j]
            if y == 0 or y == ny - 1:
                ends[y // (ny - 1), j, z] = v
            else:
                hidden[j, y - 1, z] = gelu(v).astype(BF16)

    conv(planes, (own, other), take)
    half = half_index()
    copies = []
    for j, slot in enumerate((half, 1 - half)):
        for d in range(n):
            c = pltpu.make_async_copy(hidden.at[j], out.at[d, slot, 1 : ny - 1], sems.at[j, d])
            c.start()
            copies.append(c)
    for c in copies:
        c.wait()


def first_ends_kernel(ends, below, above, _, out, hidden, sems):
    n, _, ny = out.shape[:3]
    half = half_index()
    copies = []
    for side, other in enumerate((below, above)):
        for j, slot in enumerate((half, 1 - half)):
            hidden[side, j] = gelu(ends[side, j] + other[1 - j]).astype(BF16)
            for d in range(n):
                c = pltpu.make_async_copy(
                    hidden.at[side, j], out.at[d, slot, side * (ny - 1)], sems.at[side, j, d]
                )
                c.start()
                copies.append(c)
    for c in copies:
        c.wait()


def second_edge_kernel(planes, own, other, outer_own, outer_other, inner_own, inner_other):
    ny = planes.shape[-4]
    half = half_index()
    outer, inner = ((ny - 1) * half, 2 - 2 * half), ((ny - 1) * (1 - half), 2 * half)
    for at, outs in ((outer, (outer_own, outer_other)), (inner, (inner_own, inner_other))):
        for w_ref, out in zip((own, other), outs):
            for z, v in enumerate(edge(planes, w_ref, *at)):
                out[z] = v


def channels_first(values):
    return jnp.stack(values, axis=1).astype(BF16)


def ends_role(y, ny):
    return half_index() if y == 0 else 1 - half_index()


def second_other_kernel(planes, w_ref, bias, v_ref, inner_edge, sent):
    ny, nz = planes.shape[-4:-2]
    n = planes.shape[0]
    partner = lax.axis_index("ch") + n - 2 * n * half_index()

    def take(_, y, values):
        is_end = y == 0 or y == ny - 1
        for z, v in enumerate(values):
            v = v + bias[...]
            if is_end:
                sent[2 + ends_role(y, ny), z] = v.astype(BF16)
            else:
                sent[y - 1, z] = (v_ref[partner, y, z].astype(F32) + v).astype(BF16)

    conv(planes, (w_ref,), take)
    for z in range(nz):
        sent[4, z] = inner_edge[z].astype(BF16)


def second_own_kernel(planes, w_ref, b_ref, v_ref, out, ends, mine, sem):
    ny, nz, co, nx = planes.shape[-4:]
    bias = jnp.broadcast_to(column(b_ref, co), (co, nx))
    me, half = lax.axis_index("ch"), half_index()

    def take(_, y, values):
        values = [v_ref[me, y, z].astype(F32) + (v + bias) for z, v in enumerate(values)]
        if y == 0 or y == ny - 1:
            for z, v in enumerate(values):
                ends[ends_role(y, ny), z] = v
        else:
            mine[:, y - 1] = channels_first(values)

    conv(planes, (w_ref,), take)
    copy = pltpu.make_async_copy(mine, out.at[:, pl.ds(half * ny + 1, ny - 2)], sem)
    copy.start()
    copy.wait()


def outer_end_kernel(ends, across, straight, _, out, plane, sem):
    ny, half = out.shape[1] // 2, half_index()
    plane[...] = channels_first([ends[0, z] + across[z] for z in range(ends.shape[1])])
    copy = pltpu.make_async_copy(plane, out.at[:, half * ny + (ny - 1) * half], sem)
    copy.start()
    copy.wait()


def last_kernel(ends, inner_own, straight, received, cells_first, _, out, whole, rest, sems):
    nz = ends.shape[1]
    ny, half = out.shape[1] // 2, half_index()
    mine, theirs = half * ny, (1 - half) * ny
    outer, inner = (ny - 1) * half, (ny - 1) * (1 - half)

    def got(at, z):
        return received[at, z].astype(F32)

    def start(at, z):
        return cells_first[at, z].astype(F32)

    ends_at = (
        (mine + inner, lambda z: ends[1, z] + got(4, z)),
        (theirs + inner, lambda z: start(theirs + inner, z) + (got(2, z) + straight[z])),
        (theirs + outer, lambda z: start(theirs + outer, z) + (got(3, z) + inner_own[z])),
    )
    copies = []
    for y in range(ny - 2):
        whole[:, y] = channels_first([received[y, z].astype(F32) for z in range(nz)])
    copies.append(pltpu.make_async_copy(whole, out.at[:, pl.ds(theirs + 1, ny - 2)], sems.at[3]))
    copies[-1].start()
    for i, (at, value) in enumerate(ends_at):
        rest[i] = channels_first([value(z) for z in range(nz)])
        copies.append(pltpu.make_async_copy(rest.at[i], out.at[:, at], sems.at[i]))
        copies[-1].start()
    for c in copies:
        c.wait()


ANY = pl.BlockSpec(memory_space=pl.ANY)
VMEM = pl.BlockSpec(memory_space=pltpu.VMEM)
DMA = pltpu.SemaphoreType.DMA
PARAMS = pltpu.CompilerParams(vmem_limit_bytes=48 << 20)


LONG = pl.CostEstimate(flops=40_000_000_000, bytes_accessed=1_000_000, transcendentals=0)


def call(kernel, out_shape, in_specs, out_specs, scratch, **extra):
    return pl.pallas_call(
        kernel,
        out_shape=out_shape,
        in_specs=in_specs,
        out_specs=out_specs,
        scratch_shapes=scratch,
        compiler_params=PARAMS,
        name=kernel.__name__,
        **extra,
    )


def three_parts(v):
    parts = []
    for _ in range(3):
        high = lax.reduce_precision(v, 8, 7)
        parts.append(high.astype(BF16))
        v = v - high
    return parts


def per_device(volume, first_weight, first_bias, second_weight, second_bias):
    co, full, nz, nx = volume.shape
    n, length = lax.axis_size("ch"), lax.axis_size("gy")
    g, ny = n // 2, full // 2
    axes = ("gy", "ch")
    f32 = lambda *lead: jax.ShapeDtypeStruct((*lead, nz, co, nx), F32)
    bf16 = lambda *lead: jax.ShapeDtypeStruct((*lead, nz, co, nx), BF16)

    def device(row, half, x):
        return row * n + half * g + x

    def route(*moves):
        return [
            (device(row, half, x), device(row + on, there, x))
            for half, on, there in moves
            for row in range(length)
            if 0 <= row + on < length
            for x in range(g)
        ]

    to_next = route((0, 0, 1), (1, 1, 0))
    to_previous = route((1, 0, 0), (0, -1, 1))
    to_outer = route((0, -1, 0), (1, 1, 1))
    to_across = route((0, -1, 1), (1, 1, 0))
    to_partner = route((0, 0, 1), (1, 0, 0))
    weights_route = [
        (device(row ^ 2, 1 - half, x), device(row, half, x))
        for row in range(length)
        for half in range(2)
        for x in range(g)
    ]

    core = lax.axis_index("gy") % 2
    taps = 27
    weight = first_weight.reshape(taps, co, -1)
    part = (taps + 1) // 2
    fetched = lax.ppermute(
        lax.dynamic_slice_in_dim(weight, (taps - part) * core, part, axis=0), axes, weights_route
    )
    swapped = lax.ppermute(fetched, "gy", [(i, i ^ 1) for i in range(length)])
    columns = jnp.stack(three_parts(first_bias) + three_parts(second_bias), axis=1)
    slab = jnp.pad(columns, ((0, 0), (0, weight.shape[2] - 6)))
    parcel = jnp.concatenate([second_weight.reshape(weight.shape), slab[None]], axis=0)
    other_second = lax.ppermute(parcel, axes, weights_route)

    cells_first = jnp.transpose(volume, (1, 2, 0, 3))
    sent = call(spread_kernel, bf16(n, ny), [VMEM], ANY, [DMA((n,))])(cells_first)
    main = lax.all_to_all(sent, "ch", 0, 0, tiled=True)

    below, above, other_first = call(
        first_edge_kernel,
        (f32(2), f32(2), jax.ShapeDtypeStruct(weight.shape, BF16)),
        [VMEM] * 4,
        (VMEM,) * 3,
        [],
    )(main, first_weight, fetched, swapped)
    lower = lax.ppermute(above, axes, to_next)
    upper = lax.ppermute(below, axes, to_previous)
    hidden, ends, other_bias = call(
        first_kernel,
        (bf16(g, 2, ny), f32(2, 2), jax.ShapeDtypeStruct((co, nx), F32)),
        [VMEM] * 5,
        (ANY, VMEM, VMEM),
        [pltpu.VMEM((2, ny - 2, nz, co, nx), BF16), DMA((2, g))],
    )(main, first_weight, other_first, other_second, first_bias[None])
    hidden = call(
        first_ends_kernel,
        bf16(g, 2, ny),
        [VMEM] * 3 + [ANY],
        ANY,
        [pltpu.VMEM((2, 2, nz, co, nx), BF16), DMA((2, 2, g))],
        input_output_aliases={3: 0},
    )(ends, lower, upper, hidden)

    groups = [list(range(g)), list(range(g, n))]
    gathered = lax.all_to_all(hidden, "ch", 0, 0, tiled=True, axis_index_groups=groups)

    outer_own, outer_other, inner_own, inner_other = call(
        second_edge_kernel, (f32(),) * 4, [VMEM] * 3, (VMEM,) * 4, []
    )(gathered, second_weight, other_second)
    straight = lax.ppermute(outer_own, axes, to_outer)
    across = lax.ppermute(outer_other, axes, to_across)
    out_type = jax.ShapeDtypeStruct(volume.shape, BF16)
    sent = call(second_other_kernel, bf16(5), [VMEM] * 5, VMEM, [])(
        gathered, other_second, other_bias, main, inner_other
    )
    received = lax.ppermute(sent, axes, to_partner)
    out, ends = call(
        second_own_kernel,
        (out_type, f32(2)),
        [VMEM] * 4,
        (ANY, VMEM),
        [pltpu.VMEM((co, ny - 2, nz, nx), BF16), DMA],
        cost_estimate=LONG,
    )(gathered, second_weight, second_bias[None], main)
    out = call(
        outer_end_kernel,
        out_type,
        [VMEM, VMEM, ANY, ANY],
        ANY,
        [pltpu.VMEM((co, nz, nx), BF16), DMA],
        input_output_aliases={3: 0},
        cost_estimate=LONG,
    )(ends, across, straight, out)
    return call(
        last_kernel,
        out_type,
        [VMEM] * 5 + [ANY],
        ANY,
        [pltpu.VMEM((co, ny - 2, nz, nx), BF16), pltpu.VMEM((3, co, nz, nx), BF16), DMA((4,))],
        input_output_aliases={5: 0},
    )(ends, inner_own, straight, received, cells_first, out)


def solution(mesh):
    in_specs = (
        P("ch", "gy", None, None),
        P(None, None, None, "ch", None),
        P("ch"),
        P(None, None, None, "ch", None),
        P("ch"),
    )
    out_specs = P("ch", "gy", None, None)
    return jax.shard_map(
        per_device, mesh=mesh, in_specs=in_specs, out_specs=out_specs, check_vma=False
    )
```

```python
import math

import jax
import jax.numpy as jnp
import numpy as np
from jax import lax
from jax.experimental import pallas as pl
from jax.experimental.pallas import tpu as pltpu
from jax.sharding import PartitionSpec as P

ROOT_HALF = np.float32(np.sqrt(0.5))
F32, BF16 = jnp.float32, jnp.bfloat16


def column(row_ref, n):
    i = lax.broadcasted_iota(jnp.int32, (n, n), 0)
    j = lax.broadcasted_iota(jnp.int32, (n, n), 1)
    square = jnp.where(i == j, jnp.broadcast_to(row_ref[...], (n, n)), 0.0)
    return jnp.sum(square, axis=1, keepdims=True)


def gelu(v):
    return 0.5 * v * (1.0 + lax.erf(v * ROOT_HALF))


def x_taps(a, co, nx):
    lane = lax.broadcasted_iota(jnp.int32, (co, nx), 1)
    left = jnp.where(lane == 0, 0.0, pltpu.roll(a[:co], 1, 1))
    right = jnp.where(lane == nx - 1, 0.0, pltpu.roll(a[2 * co :], nx - 1, 1))
    return a[co : 2 * co] + left + right


def z_taps(parts, co):
    nz = len(parts)
    sums = [None] * nz
    for zz in range(nz):
        for dz in range(3):
            z = zz - dz + 1
            if 0 <= z < nz:
                e = parts[zz][dz * 3 * co : (dz + 1) * 3 * co]
                sums[z] = e if sums[z] is None else sums[z] + e
    return sums


def rows(w_ref, dy):
    k = w_ref.shape[-1]
    if len(w_ref.shape) == 5:
        return w_ref[dy].reshape(-1, k)
    return w_ref[pl.ds(9 * dy, 9)].reshape(-1, k)


def cells(planes, p, z):
    lead, nx = planes.shape[:-4], planes.shape[-1]
    if len(lead) == 1:
        return planes[:, p, z].reshape(-1, nx)
    return jnp.concatenate([planes[:, a, p, z].reshape(-1, nx) for a in range(lead[1])], axis=0)


def edge(planes, w_ref, p, dy):
    nz, co, nx = planes.shape[-3:]
    parts = [
        jnp.dot(rows(w_ref, dy), cells(planes, p, zz), preferred_element_type=F32)
        for zz in range(nz)
    ]
    return [x_taps(s, co, nx) for s in z_taps(parts, co)]


def half_cells(planes):
    ny, nx = planes.shape[-4], planes.shape[-1]

    def tile(p, z):
        if 0 <= p < ny:
            return cells(planes, p, z)
        return jnp.zeros((math.prod(planes.shape[:-4]) * planes.shape[-2], nx), BF16)

    return tile


def wider_cells(planes):
    ny, half = planes.shape[-4] - 1, half_index()

    def tile(p, z):
        if 0 <= p < ny:
            return cells(planes, p + half, z)
        v = cells(planes, max(p, 0), z)
        return jnp.where(half == (1 if p < 0 else 0), v, jnp.zeros_like(v))

    return tile


def conv(tile, ny, planes, weights, take):
    nz, co, nx = planes.shape[-3:]
    half = ny // 2
    for q in range(half):
        parts = [[] for _ in weights]
        for zz in range(nz):
            tiles = []
            for dy in range(3):
                pair = [q + dy - 1, q + dy - 1 + half]
                tiles.append(jnp.concatenate([tile(p, zz) for p in pair], axis=1))
            for j, w_ref in enumerate(weights):
                part = None
                for dy in range(3):
                    d = jnp.dot(rows(w_ref, dy), tiles[dy], preferred_element_type=F32)
                    part = d if part is None else part + d
                parts[j].append(part)
        for j in range(len(weights)):
            sums = z_taps(parts[j], co)
            for h in range(2):
                values = [x_taps(s[:, h * nx : (h + 1) * nx], co, nx) for s in sums]
                take(j, q + h * half, values)


def parcel_bias(slab, at):
    parts = slab[:, at : at + 3].astype(F32)
    return parts[:, 0:1] + parts[:, 1:2] + parts[:, 2:3]


def half_index():
    return lax.axis_index("ch") // (lax.axis_size("ch") // 2)


def spread_kernel(planes, out, sems):
    n, ny = out.shape[:2]
    first = [0, planes.shape[0] - ny]
    copies = [
        pltpu.make_async_copy(planes.at[pl.ds(first[d // (n // 2)], ny)], out.at[d], sems.at[d])
        for d in range(n)
    ]
    for c in copies:
        c.start()
    for c in copies:
        c.wait()


def first_edge_kernel(planes, own, fetched, swapped, outer, other):
    part = fetched.shape[0]
    second = other.shape[0] - part
    core = lax.axis_index("gy") % 2
    other[pl.ds(second * core, part)] = fetched[...]
    other[pl.ds(second * (1 - core), part)] = swapped[...]
    half = half_index()
    for j, w_ref in enumerate((own, other)):
        for z, v in enumerate(edge(planes, w_ref, (planes.shape[-4] - 1) * half, 2 - 2 * half)):
            outer[j, z] = v


def first_kernel(planes, own, other, parcel, b_ref, out, ends, other_bias, hidden, sems):
    n, _, ny, nz, co, nx = out.shape
    slab = parcel[parcel.shape[0] - 1]
    biases = [column(b_ref, co), parcel_bias(slab, 0)]
    biases = [jnp.broadcast_to(b, (co, nx)) for b in biases]
    other_bias[...] = jnp.broadcast_to(parcel_bias(slab, 3), (co, nx))

    half = half_index()
    copies = []

    def take(j, y, values):
        for z, v in enumerate(values):
            v = v + biases[j]
            if y == 0 or y == ny - 1:
                ends[y // (ny - 1), j, z] = v
            hidden[j, y, z] = gelu(v).astype(BF16)

    conv(wider_cells(planes), ny, planes, (own, other), take)
    for j, slot in enumerate((half, 1 - half)):
        for d in range(n):
            c = pltpu.make_async_copy(hidden.at[j], out.at[d, slot], sems.at[j, d])
            c.start()
            copies.append(c)
    for c in copies:
        c.wait()


def first_ends_kernel(ends, outer, _, out, hidden, sems):
    n, _, ny = out.shape[:3]
    half = half_index()
    copies = []
    for j, slot in enumerate((half, 1 - half)):
        hidden[j] = gelu(ends[half, j] + outer[1 - j]).astype(BF16)
        for d in range(n):
            c = pltpu.make_async_copy(hidden.at[j], out.at[d, slot, (ny - 1) * half], sems.at[j, d])
            c.start()
            copies.append(c)
    for c in copies:
        c.wait()


def outer_edge(planes):
    half = half_index()
    return (planes.shape[-4] - 1) * half, 2 - 2 * half


def inner_edge(planes):
    half = half_index()
    return (planes.shape[-4] - 1) * (1 - half), 2 * half


def second_edge_kernel(planes, own, other, outer):
    for j, w_ref in enumerate((own, other)):
        for z, v in enumerate(edge(planes, w_ref, *outer_edge(planes))):
            outer[j, z] = v


def channels_first(values):
    return jnp.stack(values, axis=1).astype(BF16)


def ends_role(y, ny):
    return half_index() if y == 0 else 1 - half_index()


def second_other_kernel(planes, w_ref, bias, v_ref, sent, ends):
    ny = planes.shape[-4]
    n = planes.shape[0]
    half = half_index()
    partner = lax.axis_index("ch") + n - 2 * n * half

    def take(_, y, values):
        for z, v in enumerate(values):
            v = v + bias[...]
            whole = v_ref[partner, y + half, z].astype(F32) + v
            if y == 0 or y == ny - 1:
                role = ends_role(y, ny)
                sent[2 + role, z] = v.astype(BF16)
                ends[role, z] = whole
            else:
                sent[y - 1, z] = whole.astype(BF16)

    conv(half_cells(planes), ny, planes, (w_ref,), take)
    for z, v in enumerate(edge(planes, w_ref, *inner_edge(planes))):
        sent[4, z] = v.astype(BF16)


def finish_kernel(ends, outer, _, sent):
    sent[2] = (ends[0] + outer[0]).astype(BF16)


def second_own_kernel(planes, w_ref, b_ref, v_ref, out, ends, inner_own, mine, sem):
    ny, nz, co, nx = planes.shape[-4:]
    bias = jnp.broadcast_to(column(b_ref, co), (co, nx))
    me, half = lax.axis_index("ch"), half_index()

    def take(_, y, values):
        values = [v_ref[me, y + half, z].astype(F32) + (v + bias) for z, v in enumerate(values)]
        if y == 0 or y == ny - 1:
            for z, v in enumerate(values):
                ends[ends_role(y, ny), z] = v
        else:
            mine[:, y - 1] = channels_first(values)

    conv(half_cells(planes), ny, planes, (w_ref,), take)
    copy = pltpu.make_async_copy(mine, out.at[:, pl.ds(half * ny + 1, ny - 2)], sem)
    copy.start()
    for z, v in enumerate(edge(planes, w_ref, *inner_edge(planes))):
        inner_own[z] = v
    copy.wait()


def outer_end_kernel(ends, outer, _, out, plane, sem):
    ny, half = out.shape[1] // 2, half_index()
    plane[...] = channels_first([ends[0, z] + outer[1, z] for z in range(ends.shape[1])])
    copy = pltpu.make_async_copy(plane, out.at[:, half * ny + (ny - 1) * half], sem)
    copy.start()
    copy.wait()


def last_kernel(ends, inner_own, received, cells_first, _, out, whole, rest, sems):
    nz = ends.shape[1]
    ny, half = out.shape[1] // 2, half_index()
    mine, theirs = half * ny, (1 - half) * ny
    outer, inner = (ny - 1) * half, (ny - 1) * (1 - half)

    def got(at, z):
        return received[at, z].astype(F32)

    def start(at, z):
        return cells_first[at, z].astype(F32)

    ends_at = (
        (mine + inner, lambda z: ends[1, z] + got(4, z)),
        (theirs + inner, lambda z: got(2, z)),
        (theirs + outer, lambda z: start(theirs + outer, z) + (got(3, z) + inner_own[z])),
    )
    copies = []
    for y in range(ny - 2):
        whole[:, y] = channels_first([received[y, z].astype(F32) for z in range(nz)])
    copies.append(pltpu.make_async_copy(whole, out.at[:, pl.ds(theirs + 1, ny - 2)], sems.at[3]))
    copies[-1].start()
    for i, (at, value) in enumerate(ends_at):
        rest[i] = channels_first([value(z) for z in range(nz)])
        copies.append(pltpu.make_async_copy(rest.at[i], out.at[:, at], sems.at[i]))
        copies[-1].start()
    for c in copies:
        c.wait()


ANY = pl.BlockSpec(memory_space=pl.ANY)
VMEM = pl.BlockSpec(memory_space=pltpu.VMEM)
DMA = pltpu.SemaphoreType.DMA
PARAMS = pltpu.CompilerParams(vmem_limit_bytes=48 << 20)


LONG = pl.CostEstimate(flops=40_000_000_000, bytes_accessed=1_000_000, transcendentals=0)


def call(kernel, out_shape, in_specs, out_specs, scratch, **extra):
    return pl.pallas_call(
        kernel,
        out_shape=out_shape,
        in_specs=in_specs,
        out_specs=out_specs,
        scratch_shapes=scratch,
        compiler_params=PARAMS,
        name=kernel.__name__,
        **extra,
    )


def three_parts(v):
    parts = []
    for _ in range(3):
        high = lax.reduce_precision(v, 8, 7)
        parts.append(high.astype(BF16))
        v = v - high
    return parts


def per_device(volume, first_weight, first_bias, second_weight, second_bias):
    co, full, nz, nx = volume.shape
    n, length = lax.axis_size("ch"), lax.axis_size("gy")
    g, ny = n // 2, full // 2
    axes = ("gy", "ch")
    f32 = lambda *lead: jax.ShapeDtypeStruct((*lead, nz, co, nx), F32)
    bf16 = lambda *lead: jax.ShapeDtypeStruct((*lead, nz, co, nx), BF16)

    def device(row, half, x):
        return row * n + half * g + x

    def route(*moves):
        return [
            (device(row, half, x), device(row + on, there, x))
            for half, on, there in moves
            for row in range(length)
            if 0 <= row + on < length
            for x in range(g)
        ]

    to_across = route((0, -1, 1), (1, 1, 0))
    to_partner = route((0, 0, 1), (1, 0, 0))
    weights_route = [
        (device(row ^ 2, 1 - half, x), device(row, half, x))
        for row in range(length)
        for half in range(2)
        for x in range(g)
    ]

    core = lax.axis_index("gy") % 2
    taps = 27
    weight = first_weight.reshape(taps, co, -1)
    part = (taps + 1) // 2
    fetched = lax.ppermute(
        lax.dynamic_slice_in_dim(weight, (taps - part) * core, part, axis=0), axes, weights_route
    )
    swapped = lax.ppermute(fetched, "gy", [(i, i ^ 1) for i in range(length)])
    columns = jnp.stack(three_parts(first_bias) + three_parts(second_bias), axis=1)
    slab = jnp.pad(columns, ((0, 0), (0, weight.shape[2] - 6)))
    parcel = jnp.concatenate([second_weight.reshape(weight.shape), slab[None]], axis=0)
    other_second = lax.ppermute(parcel, axes, weights_route)

    cells_first = jnp.transpose(volume, (1, 2, 0, 3))
    sent = call(spread_kernel, bf16(n, ny + 1), [VMEM], ANY, [DMA((n,))])(cells_first)
    main = lax.all_to_all(sent, "ch", 0, 0, tiled=True)

    outer, other_first = call(
        first_edge_kernel,
        (f32(2), jax.ShapeDtypeStruct(weight.shape, BF16)),
        [VMEM] * 4,
        (VMEM,) * 2,
        [],
    )(main, first_weight, fetched, swapped)
    outer = lax.ppermute(outer, axes, to_across)
    hidden, ends, other_bias = call(
        first_kernel,
        (bf16(g, 2, ny), f32(2, 2), jax.ShapeDtypeStruct((co, nx), F32)),
        [VMEM] * 5,
        (ANY, VMEM, VMEM),
        [pltpu.VMEM((2, ny, nz, co, nx), BF16), DMA((2, g))],
    )(main, first_weight, other_first, other_second, first_bias[None])
    hidden = call(
        first_ends_kernel,
        bf16(g, 2, ny),
        [VMEM] * 2 + [ANY],
        ANY,
        [pltpu.VMEM((2, nz, co, nx), BF16), DMA((2, g))],
        input_output_aliases={2: 0},
    )(ends, outer, hidden)

    groups = [list(range(g)), list(range(g, n))]
    gathered = lax.all_to_all(hidden, "ch", 0, 0, tiled=True, axis_index_groups=groups)

    outer = call(second_edge_kernel, f32(2), [VMEM] * 3, VMEM, [])(
        gathered, second_weight, other_second
    )
    outer = lax.ppermute(outer, axes, to_across)
    out_type = jax.ShapeDtypeStruct(volume.shape, BF16)
    sent, ends = call(second_other_kernel, (bf16(5), f32(2)), [VMEM] * 4, (VMEM, VMEM), [])(
        gathered, other_second, other_bias, main
    )
    sent = call(finish_kernel, bf16(5), [VMEM] * 3, VMEM, [], input_output_aliases={2: 0})(
        ends, outer, sent
    )
    received = lax.ppermute(sent, axes, to_partner)
    out, ends, inner_own = call(
        second_own_kernel,
        (out_type, f32(2), f32()),
        [VMEM] * 4,
        (ANY, VMEM, VMEM),
        [pltpu.VMEM((co, ny - 2, nz, nx), BF16), DMA],
    )(gathered, second_weight, second_bias[None], main)
    out = call(
        outer_end_kernel,
        out_type,
        [VMEM, VMEM, ANY],
        ANY,
        [pltpu.VMEM((co, nz, nx), BF16), DMA],
        input_output_aliases={2: 0},
    )(ends, outer, out)
    return call(
        last_kernel,
        out_type,
        [VMEM] * 4 + [ANY],
        ANY,
        [pltpu.VMEM((co, ny - 2, nz, nx), BF16), pltpu.VMEM((3, co, nz, nx), BF16), DMA((4,))],
        input_output_aliases={4: 0},
    )(ends, inner_own, received, cells_first, out)


def solution(mesh):
    in_specs = (
        P("ch", "gy", None, None),
        P(None, None, None, "ch", None),
        P("ch"),
        P(None, None, None, "ch", None),
        P("ch"),
    )
    out_specs = P("ch", "gy", None, None)
    return jax.shard_map(
        per_device, mesh=mesh, in_specs=in_specs, out_specs=out_specs, check_vma=False
    )
```

```python
import math

import jax
import jax.numpy as jnp
import numpy as np
from jax import lax
from jax.experimental import pallas as pl
from jax.experimental.pallas import tpu as pltpu
from jax.sharding import PartitionSpec as P

ROOT_HALF = np.float32(np.sqrt(0.5))
F32, BF16 = jnp.float32, jnp.bfloat16


def column(row_ref, n):
    i = lax.broadcasted_iota(jnp.int32, (n, n), 0)
    j = lax.broadcasted_iota(jnp.int32, (n, n), 1)
    square = jnp.where(i == j, jnp.broadcast_to(row_ref[...], (n, n)), 0.0)
    return jnp.sum(square, axis=1, keepdims=True)


def gelu(v):
    return 0.5 * v * (1.0 + lax.erf(v * ROOT_HALF))


def x_taps(a, co, nx):
    lane = lax.broadcasted_iota(jnp.int32, (co, nx), 1)
    left = jnp.where(lane == 0, 0.0, pltpu.roll(a[:co], 1, 1))
    right = jnp.where(lane == nx - 1, 0.0, pltpu.roll(a[2 * co :], nx - 1, 1))
    return a[co : 2 * co] + left + right


def z_taps(parts, co):
    nz = len(parts)
    sums = [None] * nz
    for zz in range(nz):
        for dz in range(3):
            z = zz - dz + 1
            if 0 <= z < nz:
                e = parts[zz][dz * 3 * co : (dz + 1) * 3 * co]
                sums[z] = e if sums[z] is None else sums[z] + e
    return sums


def rows(w_ref, dy):
    k = w_ref.shape[-1]
    if len(w_ref.shape) == 5:
        return w_ref[dy].reshape(-1, k)
    return w_ref[pl.ds(9 * dy, 9)].reshape(-1, k)


def cells(planes, p, z):
    lead, nx = planes.shape[:-4], planes.shape[-1]
    if len(lead) == 1:
        return planes[:, p, z].reshape(-1, nx)
    return jnp.concatenate([planes[:, a, p, z].reshape(-1, nx) for a in range(lead[1])], axis=0)


def edge(planes, w_ref, p, dy):
    nz, co, nx = planes.shape[-3:]
    parts = [
        jnp.dot(rows(w_ref, dy), cells(planes, p, zz), preferred_element_type=F32)
        for zz in range(nz)
    ]
    return [x_taps(s, co, nx) for s in z_taps(parts, co)]


def half_cells(planes):
    ny, nx = planes.shape[-4], planes.shape[-1]

    def tile(p, z):
        if 0 <= p < ny:
            return cells(planes, p, z)
        return jnp.zeros((math.prod(planes.shape[:-4]) * planes.shape[-2], nx), BF16)

    return tile


def wider_cells(planes):
    ny, half = planes.shape[-4] - 1, half_index()

    def tile(p, z):
        if 0 <= p < ny:
            return cells(planes, p + half, z)
        v = cells(planes, max(p, 0), z)
        return jnp.where(half == (1 if p < 0 else 0), v, jnp.zeros_like(v))

    return tile


def conv(tile, ny, planes, weights, take):
    nz, co, nx = planes.shape[-3:]
    half = ny // 2
    for q in range(half):
        parts = [[] for _ in weights]
        for zz in range(nz):
            tiles = []
            for dy in range(3):
                pair = [q + dy - 1, q + dy - 1 + half]
                tiles.append(jnp.concatenate([tile(p, zz) for p in pair], axis=1))
            for j, w_ref in enumerate(weights):
                part = None
                for dy in range(3):
                    d = jnp.dot(rows(w_ref, dy), tiles[dy], preferred_element_type=F32)
                    part = d if part is None else part + d
                parts[j].append(part)
        for j in range(len(weights)):
            sums = z_taps(parts[j], co)
            for h in range(2):
                values = [x_taps(s[:, h * nx : (h + 1) * nx], co, nx) for s in sums]
                take(j, q + h * half, values)


def parcel_bias(slab, at):
    parts = slab[:, at : at + 3].astype(F32)
    return parts[:, 0:1] + parts[:, 1:2] + parts[:, 2:3]


def half_index():
    return lax.axis_index("ch") // (lax.axis_size("ch") // 2)


def spread_kernel(planes, out, sems):
    n, ny = out.shape[:2]
    first = [0, planes.shape[0] - ny]
    copies = [
        pltpu.make_async_copy(planes.at[pl.ds(first[d // (n // 2)], ny)], out.at[d], sems.at[d])
        for d in range(n)
    ]
    for c in copies:
        c.start()
    for c in copies:
        c.wait()


def first_edge_kernel(planes, own, fetched, swapped, outer, other):
    part = fetched.shape[0]
    second = other.shape[0] - part
    core = lax.axis_index("gy") % 2
    other[pl.ds(second * core, part)] = fetched[...]
    other[pl.ds(second * (1 - core), part)] = swapped[...]
    half = half_index()
    for j, w_ref in enumerate((own, other)):
        for z, v in enumerate(edge(planes, w_ref, (planes.shape[-4] - 1) * half, 2 - 2 * half)):
            outer[j, z] = v.astype(BF16)


def first_kernel(planes, own, other, parcel, b_ref, out, ends, other_bias, hidden, sems):
    n, _, ny, nz, co, nx = out.shape
    slab = parcel[parcel.shape[0] - 1]
    biases = [column(b_ref, co), parcel_bias(slab, 0)]
    biases = [jnp.broadcast_to(b, (co, nx)) for b in biases]
    other_bias[...] = jnp.broadcast_to(parcel_bias(slab, 3), (co, nx))

    half = half_index()
    copies = []

    def take(j, y, values):
        for z, v in enumerate(values):
            v = v + biases[j]
            if y == 0 or y == ny - 1:
                ends[y // (ny - 1), j, z] = v
            hidden[j, y, z] = gelu(v).astype(BF16)

    conv(wider_cells(planes), ny, planes, (own, other), take)
    for j, slot in enumerate((half, 1 - half)):
        for d in range(n):
            c = pltpu.make_async_copy(hidden.at[j], out.at[d, slot], sems.at[j, d])
            c.start()
            copies.append(c)
    for c in copies:
        c.wait()


def first_ends_kernel(ends, outer, _, out, hidden, sems):
    n, _, ny = out.shape[:3]
    half = half_index()
    copies = []
    for j, slot in enumerate((half, 1 - half)):
        hidden[j] = gelu(ends[half, j] + outer[1 - j].astype(F32)).astype(BF16)
        for d in range(n):
            c = pltpu.make_async_copy(hidden.at[j], out.at[d, slot, (ny - 1) * half], sems.at[j, d])
            c.start()
            copies.append(c)
    for c in copies:
        c.wait()


def outer_edge(planes):
    half = half_index()
    return (planes.shape[-4] - 1) * half, 2 - 2 * half


def inner_edge(planes):
    half = half_index()
    return (planes.shape[-4] - 1) * (1 - half), 2 * half


def second_edge_kernel(planes, own, other, outer):
    for j, w_ref in enumerate((own, other)):
        for z, v in enumerate(edge(planes, w_ref, *outer_edge(planes))):
            outer[j, z] = v.astype(BF16)


def channels_first(values):
    return jnp.stack(values, axis=1).astype(BF16)


def ends_role(y, ny):
    return half_index() if y == 0 else 1 - half_index()


def second_other_kernel(planes, w_ref, bias, v_ref, sent, ends):
    ny = planes.shape[-4]
    n = planes.shape[0]
    half = half_index()
    partner = lax.axis_index("ch") + n - 2 * n * half

    def take(_, y, values):
        for z, v in enumerate(values):
            v = v + bias[...]
            whole = v_ref[partner, y + half, z].astype(F32) + v
            if y == 0 or y == ny - 1:
                role = ends_role(y, ny)
                sent[2 + role, z] = v.astype(BF16)
                ends[role, z] = whole
            else:
                sent[y - 1, z] = whole.astype(BF16)

    conv(half_cells(planes), ny, planes, (w_ref,), take)
    for z, v in enumerate(edge(planes, w_ref, *inner_edge(planes))):
        sent[4, z] = v.astype(BF16)


def finish_kernel(ends, outer, _, sent):
    sent[2] = (ends[0] + outer[0].astype(F32)).astype(BF16)


def second_own_kernel(planes, w_ref, b_ref, v_ref, out, ends, inner_own, mine, sem):
    ny, nz, co, nx = planes.shape[-4:]
    bias = jnp.broadcast_to(column(b_ref, co), (co, nx))
    me, half = lax.axis_index("ch"), half_index()

    def take(_, y, values):
        values = [v_ref[me, y + half, z].astype(F32) + (v + bias) for z, v in enumerate(values)]
        if y == 0 or y == ny - 1:
            for z, v in enumerate(values):
                ends[ends_role(y, ny), z] = v
        else:
            mine[:, y - 1] = channels_first(values)

    conv(half_cells(planes), ny, planes, (w_ref,), take)
    copy = pltpu.make_async_copy(mine, out.at[:, pl.ds(half * ny + 1, ny - 2)], sem)
    copy.start()
    for z, v in enumerate(edge(planes, w_ref, *inner_edge(planes))):
        inner_own[z] = v
    copy.wait()


def outer_end_kernel(ends, outer, _, out, plane, sem):
    ny, half = out.shape[1] // 2, half_index()
    plane[...] = channels_first([ends[0, z] + outer[1, z].astype(F32) for z in range(ends.shape[1])])
    copy = pltpu.make_async_copy(plane, out.at[:, half * ny + (ny - 1) * half], sem)
    copy.start()
    copy.wait()


def last_kernel(ends, inner_own, received, cells_first, _, out, whole, rest, sems):
    nz = ends.shape[1]
    ny, half = out.shape[1] // 2, half_index()
    mine, theirs = half * ny, (1 - half) * ny
    outer, inner = (ny - 1) * half, (ny - 1) * (1 - half)

    def got(at, z):
        return received[at, z].astype(F32)

    def start(at, z):
        return cells_first[at, z].astype(F32)

    ends_at = (
        (mine + inner, lambda z: ends[1, z] + got(4, z)),
        (theirs + inner, lambda z: got(2, z)),
        (theirs + outer, lambda z: start(theirs + outer, z) + (got(3, z) + inner_own[z])),
    )
    copies = []
    for y in range(ny - 2):
        whole[:, y] = channels_first([received[y, z].astype(F32) for z in range(nz)])
    copies.append(pltpu.make_async_copy(whole, out.at[:, pl.ds(theirs + 1, ny - 2)], sems.at[3]))
    copies[-1].start()
    for i, (at, value) in enumerate(ends_at):
        rest[i] = channels_first([value(z) for z in range(nz)])
        copies.append(pltpu.make_async_copy(rest.at[i], out.at[:, at], sems.at[i]))
        copies[-1].start()
    for c in copies:
        c.wait()


ANY = pl.BlockSpec(memory_space=pl.ANY)
VMEM = pl.BlockSpec(memory_space=pltpu.VMEM)
DMA = pltpu.SemaphoreType.DMA
PARAMS = pltpu.CompilerParams(vmem_limit_bytes=48 << 20)


LONG = pl.CostEstimate(flops=40_000_000_000, bytes_accessed=1_000_000, transcendentals=0)


def call(kernel, out_shape, in_specs, out_specs, scratch, **extra):
    return pl.pallas_call(
        kernel,
        out_shape=out_shape,
        in_specs=in_specs,
        out_specs=out_specs,
        scratch_shapes=scratch,
        compiler_params=PARAMS,
        name=kernel.__name__,
        **extra,
    )


def three_parts(v):
    parts = []
    for _ in range(3):
        high = lax.reduce_precision(v, 8, 7)
        parts.append(high.astype(BF16))
        v = v - high
    return parts


def per_device(volume, first_weight, first_bias, second_weight, second_bias):
    co, full, nz, nx = volume.shape
    n, length = lax.axis_size("ch"), lax.axis_size("gy")
    g, ny = n // 2, full // 2
    axes = ("gy", "ch")
    f32 = lambda *lead: jax.ShapeDtypeStruct((*lead, nz, co, nx), F32)
    bf16 = lambda *lead: jax.ShapeDtypeStruct((*lead, nz, co, nx), BF16)

    def device(row, half, x):
        return row * n + half * g + x

    def route(*moves):
        return [
            (device(row, half, x), device(row + on, there, x))
            for half, on, there in moves
            for row in range(length)
            if 0 <= row + on < length
            for x in range(g)
        ]

    to_across = route((0, -1, 1), (1, 1, 0))
    to_partner = route((0, 0, 1), (1, 0, 0))
    weights_route = [
        (device(row ^ 2, 1 - half, x), device(row, half, x))
        for row in range(length)
        for half in range(2)
        for x in range(g)
    ]

    core = lax.axis_index("gy") % 2
    taps = 27
    weight = first_weight.reshape(taps, co, -1)
    part = (taps + 1) // 2
    fetched = lax.ppermute(
        lax.dynamic_slice_in_dim(weight, (taps - part) * core, part, axis=0), axes, weights_route
    )
    swapped = lax.ppermute(fetched, "gy", [(i, i ^ 1) for i in range(length)])
    columns = jnp.stack(three_parts(first_bias) + three_parts(second_bias), axis=1)
    slab = jnp.pad(columns, ((0, 0), (0, weight.shape[2] - 6)))
    parcel = jnp.concatenate([second_weight.reshape(weight.shape), slab[None]], axis=0)
    other_second = lax.ppermute(parcel, axes, weights_route)

    cells_first = jnp.transpose(volume, (1, 2, 0, 3))
    sent = call(spread_kernel, bf16(n, ny + 1), [VMEM], ANY, [DMA((n,))])(cells_first)
    main = lax.all_to_all(sent, "ch", 0, 0, tiled=True)

    outer, other_first = call(
        first_edge_kernel,
        (bf16(2), jax.ShapeDtypeStruct(weight.shape, BF16)),
        [VMEM] * 4,
        (VMEM,) * 2,
        [],
    )(main, first_weight, fetched, swapped)
    outer = lax.ppermute(outer, axes, to_across)
    hidden, ends, other_bias = call(
        first_kernel,
        (bf16(g, 2, ny), f32(2, 2), jax.ShapeDtypeStruct((co, nx), F32)),
        [VMEM] * 5,
        (ANY, VMEM, VMEM),
        [pltpu.VMEM((2, ny, nz, co, nx), BF16), DMA((2, g))],
    )(main, first_weight, other_first, other_second, first_bias[None])
    hidden = call(
        first_ends_kernel,
        bf16(g, 2, ny),
        [VMEM] * 2 + [ANY],
        ANY,
        [pltpu.VMEM((2, nz, co, nx), BF16), DMA((2, g))],
        input_output_aliases={2: 0},
    )(ends, outer, hidden)

    groups = [list(range(g)), list(range(g, n))]
    gathered = lax.all_to_all(hidden, "ch", 0, 0, tiled=True, axis_index_groups=groups)

    outer = call(second_edge_kernel, bf16(2), [VMEM] * 3, VMEM, [])(
        gathered, second_weight, other_second
    )
    outer = lax.ppermute(outer, axes, to_across)
    out_type = jax.ShapeDtypeStruct(volume.shape, BF16)
    sent, ends = call(second_other_kernel, (bf16(5), f32(2)), [VMEM] * 4, (VMEM, VMEM), [])(
        gathered, other_second, other_bias, main
    )
    sent = call(finish_kernel, bf16(5), [VMEM] * 3, VMEM, [], input_output_aliases={2: 0})(
        ends, outer, sent
    )
    received = lax.ppermute(sent, axes, to_partner)
    out, ends, inner_own = call(
        second_own_kernel,
        (out_type, f32(2), f32()),
        [VMEM] * 4,
        (ANY, VMEM, VMEM),
        [pltpu.VMEM((co, ny - 2, nz, nx), BF16), DMA],
    )(gathered, second_weight, second_bias[None], main)
    out = call(
        outer_end_kernel,
        out_type,
        [VMEM, VMEM, ANY],
        ANY,
        [pltpu.VMEM((co, nz, nx), BF16), DMA],
        input_output_aliases={2: 0},
    )(ends, outer, out)
    return call(
        last_kernel,
        out_type,
        [VMEM] * 4 + [ANY],
        ANY,
        [pltpu.VMEM((co, ny - 2, nz, nx), BF16), pltpu.VMEM((3, co, nz, nx), BF16), DMA((4,))],
        input_output_aliases={4: 0},
    )(ends, inner_own, received, cells_first, out)


def solution(mesh):
    in_specs = (
        P("ch", "gy", None, None),
        P(None, None, None, "ch", None),
        P("ch"),
        P(None, None, None, "ch", None),
        P("ch"),
    )
    out_specs = P("ch", "gy", None, None)
    return jax.shard_map(
        per_device, mesh=mesh, in_specs=in_specs, out_specs=out_specs, check_vma=False
    )
```

```python
import math

import jax
import jax.numpy as jnp
import numpy as np
from jax import lax
from jax.experimental import pallas as pl
from jax.experimental.pallas import tpu as pltpu
from jax.sharding import PartitionSpec as P

ROOT_HALF = np.float32(np.sqrt(0.5))
F32, BF16 = jnp.float32, jnp.bfloat16


def column(row_ref, n):
    i = lax.broadcasted_iota(jnp.int32, (n, n), 0)
    j = lax.broadcasted_iota(jnp.int32, (n, n), 1)
    square = jnp.where(i == j, jnp.broadcast_to(row_ref[...], (n, n)), 0.0)
    return jnp.sum(square, axis=1, keepdims=True)


def gelu(v):
    return 0.5 * v * (1.0 + lax.erf(v * ROOT_HALF))


def x_taps(a, co, nx):
    lane = lax.broadcasted_iota(jnp.int32, (co, nx), 1)
    left = jnp.where(lane == 0, 0.0, pltpu.roll(a[:co], 1, 1))
    right = jnp.where(lane == nx - 1, 0.0, pltpu.roll(a[2 * co :], nx - 1, 1))
    return a[co : 2 * co] + left + right


def z_taps(parts, co):
    nz = len(parts)
    sums = [None] * nz
    for zz in range(nz):
        for dz in range(3):
            z = zz - dz + 1
            if 0 <= z < nz:
                e = parts[zz][dz * 3 * co : (dz + 1) * 3 * co]
                sums[z] = e if sums[z] is None else sums[z] + e
    return sums


def rows(w_ref, dy):
    k = w_ref.shape[-1]
    if len(w_ref.shape) == 5:
        return w_ref[dy].reshape(-1, k)
    return w_ref[pl.ds(9 * dy, 9)].reshape(-1, k)


def cells(planes, p, z):
    lead, nx = planes.shape[:-4], planes.shape[-1]
    if len(lead) == 1:
        return planes[:, p, z].reshape(-1, nx)
    return jnp.concatenate([planes[:, a, p, z].reshape(-1, nx) for a in range(lead[1])], axis=0)


def edge(planes, w_ref, p, dy):
    nz, co, nx = planes.shape[-3:]
    parts = [
        jnp.dot(rows(w_ref, dy), cells(planes, p, zz), preferred_element_type=F32)
        for zz in range(nz)
    ]
    return [x_taps(s, co, nx) for s in z_taps(parts, co)]


def half_cells(planes):
    ny, nx = planes.shape[-4], planes.shape[-1]

    def tile(p, z):
        if 0 <= p < ny:
            return cells(planes, p, z)
        return jnp.zeros((math.prod(planes.shape[:-4]) * planes.shape[-2], nx), BF16)

    return tile


def wider_cells(planes):
    ny, half = planes.shape[-4] - 1, half_index()

    def tile(p, z):
        if 0 <= p < ny:
            return cells(planes, p + half, z)
        v = cells(planes, max(p, 0), z)
        return jnp.where(half == (1 if p < 0 else 0), v, jnp.zeros_like(v))

    return tile


def conv(tile, ny, planes, weights, take):
    nz, co, nx = planes.shape[-3:]
    half = ny // 2
    for q in range(half):
        parts = [[] for _ in weights]
        for zz in range(nz):
            tiles = []
            for dy in range(3):
                pair = [q + dy - 1, q + dy - 1 + half]
                tiles.append(jnp.concatenate([tile(p, zz) for p in pair], axis=1))
            for j, w_ref in enumerate(weights):
                part = None
                for dy in range(3):
                    d = jnp.dot(rows(w_ref, dy), tiles[dy], preferred_element_type=F32)
                    part = d if part is None else part + d
                parts[j].append(part)
        for j in range(len(weights)):
            sums = z_taps(parts[j], co)
            for h in range(2):
                values = [x_taps(s[:, h * nx : (h + 1) * nx], co, nx) for s in sums]
                take(j, q + h * half, values)


def parcel_bias(slab, at):
    parts = slab[:, at : at + 3].astype(F32)
    return parts[:, 0:1] + parts[:, 1:2] + parts[:, 2:3]


def half_index():
    return lax.axis_index("ch") // (lax.axis_size("ch") // 2)


def spread_kernel(planes, out, sems):
    n, ny = out.shape[:2]
    first = [0, planes.shape[0] - ny]
    copies = [
        pltpu.make_async_copy(planes.at[pl.ds(first[d // (n // 2)], ny)], out.at[d], sems.at[d])
        for d in range(n)
    ]
    for c in copies:
        c.start()
    for c in copies:
        c.wait()


def first_edge_kernel(planes, own, fetched, swapped, outer, other):
    part = fetched.shape[0]
    second = other.shape[0] - part
    core = lax.axis_index("gy") % 2
    other[pl.ds(second * core, part)] = fetched[...]
    other[pl.ds(second * (1 - core), part)] = swapped[...]
    half = half_index()
    for j, w_ref in enumerate((own, other)):
        for z, v in enumerate(edge(planes, w_ref, (planes.shape[-4] - 1) * half, 2 - 2 * half)):
            outer[j, z] = v


def first_kernel(planes, own, other, parcel, b_ref, out, ends, other_bias, hidden, sems):
    n, _, ny, nz, co, nx = out.shape
    slab = parcel[parcel.shape[0] - 1]
    biases = [column(b_ref, co), parcel_bias(slab, 0)]
    biases = [jnp.broadcast_to(b, (co, nx)) for b in biases]
    other_bias[...] = jnp.broadcast_to(parcel_bias(slab, 3), (co, nx))

    half = half_index()
    copies = []

    def take(j, y, values):
        for z, v in enumerate(values):
            v = v + biases[j]
            if y == 0 or y == ny - 1:
                ends[y // (ny - 1), j, z] = v
            hidden[j, y, z] = gelu(v).astype(BF16)

    conv(wider_cells(planes), ny, planes, (own, other), take)
    for j, slot in enumerate((half, 1 - half)):
        for d in range(n):
            c = pltpu.make_async_copy(hidden.at[j], out.at[d, slot], sems.at[j, d])
            c.start()
            copies.append(c)
    for c in copies:
        c.wait()


def first_ends_kernel(ends, outer, _, out, hidden, sems):
    n, _, ny = out.shape[:3]
    half = half_index()
    copies = []
    for j, slot in enumerate((half, 1 - half)):
        hidden[j] = gelu(ends[half, j] + outer[1 - j]).astype(BF16)
        for d in range(n):
            c = pltpu.make_async_copy(hidden.at[j], out.at[d, slot, (ny - 1) * half], sems.at[j, d])
            c.start()
            copies.append(c)
    for c in copies:
        c.wait()


def outer_edge(planes):
    half = half_index()
    return (planes.shape[-4] - 1) * half, 2 - 2 * half


def inner_edge(planes):
    half = half_index()
    return (planes.shape[-4] - 1) * (1 - half), 2 * half


def second_edge_kernel(planes, own, other, outer):
    for j, w_ref in enumerate((own, other)):
        for z, v in enumerate(edge(planes, w_ref, *outer_edge(planes))):
            outer[j, z] = v


def channels_first(values):
    return jnp.stack(values, axis=1).astype(BF16)


def ends_role(y, ny):
    return half_index() if y == 0 else 1 - half_index()


def two_parts(v):
    high = v.astype(BF16)
    return high, (v - high.astype(F32)).astype(BF16)


def second_other_kernel(planes, w_ref, bias, v_ref, sent, ends):
    ny = planes.shape[-4]
    n = planes.shape[0]
    half = half_index()
    partner = lax.axis_index("ch") + n - 2 * n * half

    def take(_, y, values):
        for z, v in enumerate(values):
            v = v + bias[...]
            whole = v_ref[partner, y + half, z].astype(F32) + v
            if y == 0 or y == ny - 1:
                ends[ends_role(y, ny), z] = whole
            else:
                sent[y - 1, z] = whole.astype(BF16)

    conv(half_cells(planes), ny, planes, (w_ref,), take)
    for z, v in enumerate(edge(planes, w_ref, *inner_edge(planes))):
        sent[5, z], sent[6, z] = two_parts(v)


def finish_kernel(ends, outer, _, sent):
    sent[2] = (ends[0] + outer[0]).astype(BF16)
    sent[3], sent[4] = two_parts(ends[1])


def second_own_kernel(planes, w_ref, b_ref, v_ref, out, ends, inner_own, mine, sem):
    ny, nz, co, nx = planes.shape[-4:]
    bias = jnp.broadcast_to(column(b_ref, co), (co, nx))
    me, half = lax.axis_index("ch"), half_index()

    def take(_, y, values):
        values = [v_ref[me, y + half, z].astype(F32) + (v + bias) for z, v in enumerate(values)]
        if y == 0 or y == ny - 1:
            for z, v in enumerate(values):
                ends[ends_role(y, ny), z] = v
        else:
            mine[:, y - 1] = channels_first(values)

    conv(half_cells(planes), ny, planes, (w_ref,), take)
    copy = pltpu.make_async_copy(mine, out.at[:, pl.ds(half * ny + 1, ny - 2)], sem)
    copy.start()
    for z, v in enumerate(edge(planes, w_ref, *inner_edge(planes))):
        inner_own[z] = v
    copy.wait()


def outer_end_kernel(ends, outer, _, out, plane, sem):
    ny, half = out.shape[1] // 2, half_index()
    plane[...] = channels_first([ends[0, z] + outer[1, z] for z in range(ends.shape[1])])
    copy = pltpu.make_async_copy(plane, out.at[:, half * ny + (ny - 1) * half], sem)
    copy.start()
    copy.wait()


def last_kernel(ends, inner_own, received, _, out, whole, rest, sems):
    nz = ends.shape[1]
    ny, half = out.shape[1] // 2, half_index()
    mine, theirs = half * ny, (1 - half) * ny
    outer, inner = (ny - 1) * half, (ny - 1) * (1 - half)

    def got(at, z):
        return received[at, z].astype(F32)

    ends_at = (
        (mine + inner, lambda z: ends[1, z] + (got(5, z) + got(6, z))),
        (theirs + inner, lambda z: got(2, z)),
        (theirs + outer, lambda z: (got(3, z) + got(4, z)) + inner_own[z]),
    )
    copies = []
    for y in range(ny - 2):
        whole[:, y] = channels_first([received[y, z].astype(F32) for z in range(nz)])
    copies.append(pltpu.make_async_copy(whole, out.at[:, pl.ds(theirs + 1, ny - 2)], sems.at[3]))
    copies[-1].start()
    for i, (at, value) in enumerate(ends_at):
        rest[i] = channels_first([value(z) for z in range(nz)])
        copies.append(pltpu.make_async_copy(rest.at[i], out.at[:, at], sems.at[i]))
        copies[-1].start()
    for c in copies:
        c.wait()


ANY = pl.BlockSpec(memory_space=pl.ANY)
VMEM = pl.BlockSpec(memory_space=pltpu.VMEM)
DMA = pltpu.SemaphoreType.DMA
PARAMS = pltpu.CompilerParams(vmem_limit_bytes=48 << 20)


LONG = pl.CostEstimate(flops=40_000_000_000, bytes_accessed=1_000_000, transcendentals=0)


def call(kernel, out_shape, in_specs, out_specs, scratch, **extra):
    return pl.pallas_call(
        kernel,
        out_shape=out_shape,
        in_specs=in_specs,
        out_specs=out_specs,
        scratch_shapes=scratch,
        compiler_params=PARAMS,
        name=kernel.__name__,
        **extra,
    )


def three_parts(v):
    parts = []
    for _ in range(3):
        high = lax.reduce_precision(v, 8, 7)
        parts.append(high.astype(BF16))
        v = v - high
    return parts


def per_device(volume, first_weight, first_bias, second_weight, second_bias):
    co, full, nz, nx = volume.shape
    n, length = lax.axis_size("ch"), lax.axis_size("gy")
    g, ny = n // 2, full // 2
    axes = ("gy", "ch")
    f32 = lambda *lead: jax.ShapeDtypeStruct((*lead, nz, co, nx), F32)
    bf16 = lambda *lead: jax.ShapeDtypeStruct((*lead, nz, co, nx), BF16)

    def device(row, half, x):
        return row * n + half * g + x

    def route(*moves):
        return [
            (device(row, half, x), device(row + on, there, x))
            for half, on, there in moves
            for row in range(length)
            if 0 <= row + on < length
            for x in range(g)
        ]

    to_across = route((0, -1, 1), (1, 1, 0))
    to_partner = route((0, 0, 1), (1, 0, 0))
    weights_route = [
        (device(row ^ 2, 1 - half, x), device(row, half, x))
        for row in range(length)
        for half in range(2)
        for x in range(g)
    ]

    core = lax.axis_index("gy") % 2
    taps = 27
    weight = first_weight.reshape(taps, co, -1)
    part = (taps + 1) // 2
    fetched = lax.ppermute(
        lax.dynamic_slice_in_dim(weight, (taps - part) * core, part, axis=0), axes, weights_route
    )
    swapped = lax.ppermute(fetched, "gy", [(i, i ^ 1) for i in range(length)])
    columns = jnp.stack(three_parts(first_bias) + three_parts(second_bias), axis=1)
    slab = jnp.pad(columns, ((0, 0), (0, weight.shape[2] - 6)))
    parcel = jnp.concatenate([second_weight.reshape(weight.shape), slab[None]], axis=0)
    other_second = lax.ppermute(parcel, axes, weights_route)

    cells_first = jnp.transpose(volume, (1, 2, 0, 3))
    sent = call(spread_kernel, bf16(n, ny + 1), [VMEM], ANY, [DMA((n,))])(cells_first)
    main = lax.all_to_all(sent, "ch", 0, 0, tiled=True)

    outer, other_first = call(
        first_edge_kernel,
        (f32(2), jax.ShapeDtypeStruct(weight.shape, BF16)),
        [VMEM] * 4,
        (VMEM,) * 2,
        [],
    )(main, first_weight, fetched, swapped)
    outer = lax.ppermute(outer, axes, to_across)
    hidden, ends, other_bias = call(
        first_kernel,
        (bf16(g, 2, ny), f32(2, 2), jax.ShapeDtypeStruct((co, nx), F32)),
        [VMEM] * 5,
        (ANY, VMEM, VMEM),
        [pltpu.VMEM((2, ny, nz, co, nx), BF16), DMA((2, g))],
    )(main, first_weight, other_first, other_second, first_bias[None])
    hidden = call(
        first_ends_kernel,
        bf16(g, 2, ny),
        [VMEM] * 2 + [ANY],
        ANY,
        [pltpu.VMEM((2, nz, co, nx), BF16), DMA((2, g))],
        input_output_aliases={2: 0},
    )(ends, outer, hidden)

    groups = [list(range(g)), list(range(g, n))]
    gathered = lax.all_to_all(hidden, "ch", 0, 0, tiled=True, axis_index_groups=groups)

    outer = call(second_edge_kernel, f32(2), [VMEM] * 3, VMEM, [])(
        gathered, second_weight, other_second
    )
    outer = lax.ppermute(outer, axes, to_across)
    out_type = jax.ShapeDtypeStruct(volume.shape, BF16)
    sent, ends = call(second_other_kernel, (bf16(7), f32(2)), [VMEM] * 4, (VMEM, VMEM), [])(
        gathered, other_second, other_bias, main
    )
    sent = call(finish_kernel, bf16(7), [VMEM] * 3, VMEM, [], input_output_aliases={2: 0})(
        ends, outer, sent
    )
    received = lax.ppermute(sent, axes, to_partner)
    out, ends, inner_own = call(
        second_own_kernel,
        (out_type, f32(2), f32()),
        [VMEM] * 4,
        (ANY, VMEM, VMEM),
        [pltpu.VMEM((co, ny - 2, nz, nx), BF16), DMA],
    )(gathered, second_weight, second_bias[None], main)
    out = call(
        outer_end_kernel,
        out_type,
        [VMEM, VMEM, ANY],
        ANY,
        [pltpu.VMEM((co, nz, nx), BF16), DMA],
        input_output_aliases={2: 0},
    )(ends, outer, out)
    return call(
        last_kernel,
        out_type,
        [VMEM] * 3 + [ANY],
        ANY,
        [pltpu.VMEM((co, ny - 2, nz, nx), BF16), pltpu.VMEM((3, co, nz, nx), BF16), DMA((4,))],
        input_output_aliases={3: 0},
    )(ends, inner_own, received, out)


def solution(mesh):
    in_specs = (
        P("ch", "gy", None, None),
        P(None, None, None, "ch", None),
        P("ch"),
        P(None, None, None, "ch", None),
        P("ch"),
    )
    out_specs = P("ch", "gy", None, None)
    return jax.shard_map(
        per_device, mesh=mesh, in_specs=in_specs, out_specs=out_specs, check_vma=False
    )
```

```python
import math

import jax
import jax.numpy as jnp
import numpy as np
from jax import lax
from jax.experimental import pallas as pl
from jax.experimental.pallas import tpu as pltpu
from jax.sharding import PartitionSpec as P

ROOT_HALF = np.float32(np.sqrt(0.5))
F32, BF16 = jnp.float32, jnp.bfloat16


def column(row_ref, n):
    i = lax.broadcasted_iota(jnp.int32, (n, n), 0)
    j = lax.broadcasted_iota(jnp.int32, (n, n), 1)
    square = jnp.where(i == j, jnp.broadcast_to(row_ref[...], (n, n)), 0.0)
    return jnp.sum(square, axis=1, keepdims=True)


def gelu(v):
    return 0.5 * v * (1.0 + lax.erf(v * ROOT_HALF))


def x_taps(a, co, nx):
    lane = lax.broadcasted_iota(jnp.int32, (co, nx), 1)
    left = jnp.where(lane == 0, 0.0, pltpu.roll(a[:co], 1, 1))
    right = jnp.where(lane == nx - 1, 0.0, pltpu.roll(a[2 * co :], nx - 1, 1))
    return a[co : 2 * co] + left + right


def z_taps(parts, co):
    nz = len(parts)
    sums = [None] * nz
    for zz in range(nz):
        for dz in range(3):
            z = zz - dz + 1
            if 0 <= z < nz:
                e = parts[zz][dz * 3 * co : (dz + 1) * 3 * co]
                sums[z] = e if sums[z] is None else sums[z] + e
    return sums


def rows(w_ref, dy):
    k = w_ref.shape[-1]
    if len(w_ref.shape) == 5:
        return w_ref[dy].reshape(-1, k)
    return w_ref[pl.ds(9 * dy, 9)].reshape(-1, k)


def cells(planes, p, z):
    lead, nx = planes.shape[:-4], planes.shape[-1]
    if len(lead) == 1:
        return planes[:, p, z].reshape(-1, nx)
    return jnp.concatenate([planes[:, a, p, z].reshape(-1, nx) for a in range(lead[1])], axis=0)


def edge(planes, w_ref, p, dy):
    nz, co, nx = planes.shape[-3:]
    parts = [
        jnp.dot(rows(w_ref, dy), cells(planes, p, zz), preferred_element_type=F32)
        for zz in range(nz)
    ]
    return [x_taps(s, co, nx) for s in z_taps(parts, co)]


def half_cells(planes):
    ny, nx = planes.shape[-4], planes.shape[-1]

    def tile(p, z):
        if 0 <= p < ny:
            return cells(planes, p, z)
        return jnp.zeros((math.prod(planes.shape[:-4]) * planes.shape[-2], nx), BF16)

    return tile


def wider_cells(planes):
    ny, half = planes.shape[-4] - 1, half_index()

    def tile(p, z):
        if 0 <= p < ny:
            return cells(planes, p + half, z)
        v = cells(planes, max(p, 0), z)
        return jnp.where(half == (1 if p < 0 else 0), v, jnp.zeros_like(v))

    return tile


def conv(tile, ny, planes, weights, take):
    nz, co, nx = planes.shape[-3:]
    half = ny // 2
    for q in range(half):
        parts = [[] for _ in weights]
        for zz in range(nz):
            tiles = []
            for dy in range(3):
                pair = [q + dy - 1, q + dy - 1 + half]
                tiles.append(jnp.concatenate([tile(p, zz) for p in pair], axis=1))
            for j, w_ref in enumerate(weights):
                part = None
                for dy in range(3):
                    d = jnp.dot(rows(w_ref, dy), tiles[dy], preferred_element_type=F32)
                    part = d if part is None else part + d
                parts[j].append(part)
        for j in range(len(weights)):
            sums = z_taps(parts[j], co)
            for h in range(2):
                values = [x_taps(s[:, h * nx : (h + 1) * nx], co, nx) for s in sums]
                take(j, q + h * half, values)


def parcel_bias(slab, at):
    parts = slab[:, at : at + 3].astype(F32)
    return parts[:, 0:1] + parts[:, 1:2] + parts[:, 2:3]


def half_index():
    return lax.axis_index("ch") // (lax.axis_size("ch") // 2)


def spread_kernel(planes, out, sems):
    n, ny = out.shape[:2]
    first = [0, planes.shape[0] - ny]
    copies = [
        pltpu.make_async_copy(planes.at[pl.ds(first[d // (n // 2)], ny)], out.at[d], sems.at[d])
        for d in range(n)
    ]
    for c in copies:
        c.start()
    for c in copies:
        c.wait()


def first_edge_kernel(planes, own, fetched, swapped, outer, other):
    part = fetched.shape[0]
    second = other.shape[0] - part
    core = lax.axis_index("gy") % 2
    other[pl.ds(second * core, part)] = fetched[...]
    other[pl.ds(second * (1 - core), part)] = swapped[...]
    half = half_index()
    for j, w_ref in enumerate((own, other)):
        for z, v in enumerate(edge(planes, w_ref, (planes.shape[-4] - 1) * half, 2 - 2 * half)):
            outer[j, z] = v


def first_kernel(planes, own, other, parcel, b_ref, out, ends, other_bias, hidden, sems):
    n, _, ny, nz, co, nx = out.shape
    slab = parcel[parcel.shape[0] - 1]
    biases = [column(b_ref, co), parcel_bias(slab, 0)]
    biases = [jnp.broadcast_to(b, (co, nx)) for b in biases]
    other_bias[...] = jnp.broadcast_to(parcel_bias(slab, 3), (co, nx))

    half = half_index()
    copies = []

    def take(j, y, values):
        for z, v in enumerate(values):
            v = v + biases[j]
            if y == 0 or y == ny - 1:
                ends[y // (ny - 1), j, z] = v
            hidden[j, y, z] = gelu(v).astype(BF16)

    conv(wider_cells(planes), ny, planes, (own, other), take)
    for j, slot in enumerate((half, 1 - half)):
        for d in range(n):
            c = pltpu.make_async_copy(hidden.at[j], out.at[d, slot], sems.at[j, d])
            c.start()
            copies.append(c)
    for c in copies:
        c.wait()


def first_ends_kernel(ends, outer, _, out, hidden, sems):
    n, _, ny = out.shape[:3]
    half = half_index()
    copies = []
    for j, slot in enumerate((half, 1 - half)):
        hidden[j] = gelu(ends[half, j] + outer[1 - j]).astype(BF16)
        for d in range(n):
            c = pltpu.make_async_copy(hidden.at[j], out.at[d, slot, (ny - 1) * half], sems.at[j, d])
            c.start()
            copies.append(c)
    for c in copies:
        c.wait()


def outer_edge(planes):
    half = half_index()
    return (planes.shape[-4] - 1) * half, 2 - 2 * half


def inner_edge(planes):
    half = half_index()
    return (planes.shape[-4] - 1) * (1 - half), 2 * half


def second_edge_kernel(planes, own, other, outer):
    for j, w_ref in enumerate((own, other)):
        for z, v in enumerate(edge(planes, w_ref, *outer_edge(planes))):
            outer[j, z] = v


def channels_first(values):
    return jnp.stack(values, axis=1).astype(BF16)


def ends_role(y, ny):
    return half_index() if y == 0 else 1 - half_index()


def two_parts(v):
    high = v.astype(BF16)
    return high, (v - high.astype(F32)).astype(BF16)


def second_other_kernel(planes, w_ref, bias, v_ref, _, sent, ends):
    ny = planes.shape[-4]
    n = planes.shape[0]
    half = half_index()
    partner = lax.axis_index("ch") + n - 2 * n * half

    def take(_, y, values):
        for z, v in enumerate(values):
            v = v + bias[...]
            whole = v_ref[partner, y + half, z].astype(F32) + v
            if y == 0 or y == ny - 1:
                ends[ends_role(y, ny), z] = whole
            else:
                sent[y - 1, z] = whole.astype(BF16)

    conv(half_cells(planes), ny, planes, (w_ref,), take)
    sent[2], sent[3] = two_parts(ends[1])
    for z, v in enumerate(edge(planes, w_ref, *inner_edge(planes))):
        sent[4, z], sent[5, z] = two_parts(v)


def finish_kernel(ends, outer, sent):
    sent[...] = (ends[0] + outer[0]).astype(BF16)


def second_own_kernel(planes, w_ref, b_ref, v_ref, out, ends, inner_own, mine, sem):
    ny, nz, co, nx = planes.shape[-4:]
    bias = jnp.broadcast_to(column(b_ref, co), (co, nx))
    me, half = lax.axis_index("ch"), half_index()

    def take(_, y, values):
        values = [v_ref[me, y + half, z].astype(F32) + (v + bias) for z, v in enumerate(values)]
        if y == 0 or y == ny - 1:
            for z, v in enumerate(values):
                ends[ends_role(y, ny), z] = v
        else:
            mine[:, y - 1] = channels_first(values)

    conv(half_cells(planes), ny, planes, (w_ref,), take)
    copy = pltpu.make_async_copy(mine, out.at[:, pl.ds(half * ny + 1, ny - 2)], sem)
    copy.start()
    for z, v in enumerate(edge(planes, w_ref, *inner_edge(planes))):
        inner_own[z] = v
    copy.wait()


def outer_end_kernel(ends, outer, _, out, plane, sem):
    ny, half = out.shape[1] // 2, half_index()
    plane[...] = channels_first([ends[0, z] + outer[1, z] for z in range(ends.shape[1])])
    copy = pltpu.make_async_copy(plane, out.at[:, half * ny + (ny - 1) * half], sem)
    copy.start()
    copy.wait()


def last_kernel(ends, inner_own, received, last_plane, _, out, whole, rest, sems):
    nz = ends.shape[1]
    ny, half = out.shape[1] // 2, half_index()
    mine, theirs = half * ny, (1 - half) * ny
    outer, inner = (ny - 1) * half, (ny - 1) * (1 - half)

    def got(at, z):
        return received[at, z].astype(F32)

    ends_at = (
        (mine + inner, lambda z: ends[1, z] + (got(4, z) + got(5, z))),
        (theirs + inner, lambda z: last_plane[z].astype(F32)),
        (theirs + outer, lambda z: (got(2, z) + got(3, z)) + inner_own[z]),
    )
    copies = []
    for y in range(ny - 2):
        whole[:, y] = channels_first([received[y, z].astype(F32) for z in range(nz)])
    copies.append(pltpu.make_async_copy(whole, out.at[:, pl.ds(theirs + 1, ny - 2)], sems.at[3]))
    copies[-1].start()
    for i, (at, value) in enumerate(ends_at):
        rest[i] = channels_first([value(z) for z in range(nz)])
        copies.append(pltpu.make_async_copy(rest.at[i], out.at[:, at], sems.at[i]))
        copies[-1].start()
    for c in copies:
        c.wait()


ANY = pl.BlockSpec(memory_space=pl.ANY)
VMEM = pl.BlockSpec(memory_space=pltpu.VMEM)
DMA = pltpu.SemaphoreType.DMA
PARAMS = pltpu.CompilerParams(vmem_limit_bytes=48 << 20)


LONG = pl.CostEstimate(flops=40_000_000_000, bytes_accessed=1_000_000, transcendentals=0)


def call(kernel, out_shape, in_specs, out_specs, scratch, **extra):
    return pl.pallas_call(
        kernel,
        out_shape=out_shape,
        in_specs=in_specs,
        out_specs=out_specs,
        scratch_shapes=scratch,
        compiler_params=PARAMS,
        name=kernel.__name__,
        **extra,
    )


def three_parts(v):
    parts = []
    for _ in range(3):
        high = lax.reduce_precision(v, 8, 7)
        parts.append(high.astype(BF16))
        v = v - high
    return parts


def per_device(volume, first_weight, first_bias, second_weight, second_bias):
    co, full, nz, nx = volume.shape
    n, length = lax.axis_size("ch"), lax.axis_size("gy")
    g, ny = n // 2, full // 2
    axes = ("gy", "ch")
    f32 = lambda *lead: jax.ShapeDtypeStruct((*lead, nz, co, nx), F32)
    bf16 = lambda *lead: jax.ShapeDtypeStruct((*lead, nz, co, nx), BF16)

    def device(row, half, x):
        return row * n + half * g + x

    def route(*moves):
        return [
            (device(row, half, x), device(row + on, there, x))
            for half, on, there in moves
            for row in range(length)
            if 0 <= row + on < length
            for x in range(g)
        ]

    to_across = route((0, -1, 1), (1, 1, 0))
    to_partner = route((0, 0, 1), (1, 0, 0))
    weights_route = [
        (device(row ^ 2, 1 - half, x), device(row, half, x))
        for row in range(length)
        for half in range(2)
        for x in range(g)
    ]

    core = lax.axis_index("gy") % 2
    taps = 27
    weight = first_weight.reshape(taps, co, -1)
    part = (taps + 1) // 2
    fetched = lax.ppermute(
        lax.dynamic_slice_in_dim(weight, (taps - part) * core, part, axis=0), axes, weights_route
    )
    swapped = lax.ppermute(fetched, "gy", [(i, i ^ 1) for i in range(length)])
    columns = jnp.stack(three_parts(first_bias) + three_parts(second_bias), axis=1)
    slab = jnp.pad(columns, ((0, 0), (0, weight.shape[2] - 6)))
    parcel = jnp.concatenate([second_weight.reshape(weight.shape), slab[None]], axis=0)
    other_second = lax.ppermute(parcel, axes, weights_route)

    cells_first = jnp.transpose(volume, (1, 2, 0, 3))
    sent = call(spread_kernel, bf16(n, ny + 1), [VMEM], ANY, [DMA((n,))])(cells_first)
    main = lax.all_to_all(sent, "ch", 0, 0, tiled=True)

    outer, other_first = call(
        first_edge_kernel,
        (f32(2), jax.ShapeDtypeStruct(weight.shape, BF16)),
        [VMEM] * 4,
        (VMEM,) * 2,
        [],
    )(main, first_weight, fetched, swapped)
    outer = lax.ppermute(outer, axes, to_across)
    hidden, ends, other_bias = call(
        first_kernel,
        (bf16(g, 2, ny), f32(2, 2), jax.ShapeDtypeStruct((co, nx), F32)),
        [VMEM] * 5,
        (ANY, VMEM, VMEM),
        [pltpu.VMEM((2, ny, nz, co, nx), BF16), DMA((2, g))],
    )(main, first_weight, other_first, other_second, first_bias[None])
    hidden = call(
        first_ends_kernel,
        bf16(g, 2, ny),
        [VMEM] * 2 + [ANY],
        ANY,
        [pltpu.VMEM((2, nz, co, nx), BF16), DMA((2, g))],
        input_output_aliases={2: 0},
    )(ends, outer, hidden)

    groups = [list(range(g)), list(range(g, n))]
    gathered = lax.all_to_all(hidden, "ch", 0, 0, tiled=True, axis_index_groups=groups)

    edges = call(second_edge_kernel, f32(2), [VMEM] * 3, VMEM, [])(
        gathered, second_weight, other_second
    )
    outer = lax.ppermute(edges, axes, to_across)
    out_type = jax.ShapeDtypeStruct(volume.shape, BF16)
    sent, ends = call(second_other_kernel, (bf16(6), f32(2)), [VMEM] * 4 + [ANY], (VMEM, VMEM), [])(
        gathered, other_second, other_bias, main, edges
    )
    received = lax.ppermute(sent, axes, to_partner)
    last_plane = call(finish_kernel, bf16(), [VMEM] * 2, VMEM, [], cost_estimate=LONG)(ends, outer)
    last_plane = lax.ppermute(last_plane, axes, to_partner)
    out, ends, inner_own = call(
        second_own_kernel,
        (out_type, f32(2), f32()),
        [VMEM] * 4,
        (ANY, VMEM, VMEM),
        [pltpu.VMEM((co, ny - 2, nz, nx), BF16), DMA],
    )(gathered, second_weight, second_bias[None], main)
    out = call(
        outer_end_kernel,
        out_type,
        [VMEM, VMEM, ANY],
        ANY,
        [pltpu.VMEM((co, nz, nx), BF16), DMA],
        input_output_aliases={2: 0},
    )(ends, outer, out)
    return call(
        last_kernel,
        out_type,
        [VMEM] * 4 + [ANY],
        ANY,
        [pltpu.VMEM((co, ny - 2, nz, nx), BF16), pltpu.VMEM((3, co, nz, nx), BF16), DMA((4,))],
        input_output_aliases={4: 0},
    )(ends, inner_own, received, last_plane, out)


def solution(mesh):
    in_specs = (
        P("ch", "gy", None, None),
        P(None, None, None, "ch", None),
        P("ch"),
        P(None, None, None, "ch", None),
        P("ch"),
    )
    out_specs = P("ch", "gy", None, None)
    return jax.shard_map(
        per_device, mesh=mesh, in_specs=in_specs, out_specs=out_specs, check_vma=False
    )
```

```python
import math

import jax
import jax.numpy as jnp
import numpy as np
from jax import lax
from jax.experimental import pallas as pl
from jax.experimental.pallas import tpu as pltpu
from jax.sharding import PartitionSpec as P

ROOT_HALF = np.float32(np.sqrt(0.5))
F32, BF16 = jnp.float32, jnp.bfloat16


def column(row_ref, n):
    i = lax.broadcasted_iota(jnp.int32, (n, n), 0)
    j = lax.broadcasted_iota(jnp.int32, (n, n), 1)
    square = jnp.where(i == j, jnp.broadcast_to(row_ref[...], (n, n)), 0.0)
    return jnp.sum(square, axis=1, keepdims=True)


def gelu(v):
    return 0.5 * v * (1.0 + lax.erf(v * ROOT_HALF))


def x_taps(a, co, nx):
    lane = lax.broadcasted_iota(jnp.int32, (co, nx), 1)
    left = jnp.where(lane == 0, 0.0, pltpu.roll(a[:co], 1, 1))
    right = jnp.where(lane == nx - 1, 0.0, pltpu.roll(a[2 * co :], nx - 1, 1))
    return a[co : 2 * co] + left + right


def z_taps(parts, co):
    nz = len(parts)
    sums = [None] * nz
    for zz in range(nz):
        for dz in range(3):
            z = zz - dz + 1
            if 0 <= z < nz:
                e = parts[zz][dz * 3 * co : (dz + 1) * 3 * co]
                sums[z] = e if sums[z] is None else sums[z] + e
    return sums


def rows(w_ref, dy):
    k = w_ref.shape[-1]
    if len(w_ref.shape) == 5:
        return w_ref[dy].reshape(-1, k)
    return w_ref[pl.ds(9 * dy, 9)].reshape(-1, k)


def cells(planes, p, z):
    lead, nx = planes.shape[:-4], planes.shape[-1]
    if len(lead) == 1:
        return planes[:, p, z].reshape(-1, nx)
    return jnp.concatenate([planes[:, a, p, z].reshape(-1, nx) for a in range(lead[1])], axis=0)


def edge(planes, w_ref, p, dy):
    nz, co, nx = planes.shape[-3:]
    parts = [
        jnp.dot(rows(w_ref, dy), cells(planes, p, zz), preferred_element_type=F32)
        for zz in range(nz)
    ]
    return [x_taps(s, co, nx) for s in z_taps(parts, co)]


def half_cells(planes):
    ny, nx = planes.shape[-4], planes.shape[-1]

    def tile(p, z):
        if 0 <= p < ny:
            return cells(planes, p, z)
        return jnp.zeros((math.prod(planes.shape[:-4]) * planes.shape[-2], nx), BF16)

    return tile


def wider_cells(planes):
    ny, half = planes.shape[-4] - 1, half_index()

    def tile(p, z):
        if 0 <= p < ny:
            return cells(planes, p + half, z)
        v = cells(planes, max(p, 0), z)
        return jnp.where(half == (1 if p < 0 else 0), v, jnp.zeros_like(v))

    return tile


def conv(tile, ny, planes, weights, take):
    nz, co, nx = planes.shape[-3:]
    half = ny // 2
    for q in range(half):
        parts = [[] for _ in weights]
        for zz in range(nz):
            tiles = []
            for dy in range(3):
                pair = [q + dy - 1, q + dy - 1 + half]
                tiles.append(jnp.concatenate([tile(p, zz) for p in pair], axis=1))
            for j, w_ref in enumerate(weights):
                part = None
                for dy in range(3):
                    d = jnp.dot(rows(w_ref, dy), tiles[dy], preferred_element_type=F32)
                    part = d if part is None else part + d
                parts[j].append(part)
        for j in range(len(weights)):
            sums = z_taps(parts[j], co)
            for h in range(2):
                values = [x_taps(s[:, h * nx : (h + 1) * nx], co, nx) for s in sums]
                take(j, q + h * half, values)


def parcel_bias(slab, at):
    parts = slab[:, at : at + 3].astype(F32)
    return parts[:, 0:1] + parts[:, 1:2] + parts[:, 2:3]


def half_index():
    return lax.axis_index("ch") // (lax.axis_size("ch") // 2)


def spread_kernel(planes, out, sems):
    n, ny = out.shape[:2]
    first = [0, planes.shape[0] - ny]
    copies = [
        pltpu.make_async_copy(planes.at[pl.ds(first[d // (n // 2)], ny)], out.at[d], sems.at[d])
        for d in range(n)
    ]
    for c in copies:
        c.start()
    for c in copies:
        c.wait()


def first_edge_kernel(planes, own, fetched, swapped, outer, other):
    part = fetched.shape[0]
    second = other.shape[0] - part
    core = lax.axis_index("gy") % 2
    other[pl.ds(second * core, part)] = fetched[...]
    other[pl.ds(second * (1 - core), part)] = swapped[...]
    half = half_index()
    for j, w_ref in enumerate((own, other)):
        for z, v in enumerate(edge(planes, w_ref, (planes.shape[-4] - 1) * half, 2 - 2 * half)):
            outer[j, z] = v


def first_kernel(planes, own, other, parcel, b_ref, out, ends, other_bias, hidden, sems):
    n, _, ny, nz, co, nx = out.shape
    slab = parcel[parcel.shape[0] - 1]
    biases = [column(b_ref, co), parcel_bias(slab, 0)]
    biases = [jnp.broadcast_to(b, (co, nx)) for b in biases]
    other_bias[...] = jnp.broadcast_to(parcel_bias(slab, 3), (co, nx))

    half = half_index()
    copies = []

    def take(j, y, values):
        for z, v in enumerate(values):
            v = v + biases[j]
            if y == 0 or y == ny - 1:
                ends[y // (ny - 1), j, z] = v
            hidden[j, y, z] = gelu(v).astype(BF16)

    conv(wider_cells(planes), ny, planes, (own, other), take)
    for j, slot in enumerate((half, 1 - half)):
        for d in range(n):
            c = pltpu.make_async_copy(hidden.at[j], out.at[d, slot], sems.at[j, d])
            c.start()
            copies.append(c)
    for c in copies:
        c.wait()


def first_ends_kernel(ends, outer, _, out, hidden, sems):
    n, _, ny = out.shape[:3]
    half = half_index()
    copies = []
    for j, slot in enumerate((half, 1 - half)):
        hidden[j] = gelu(ends[half, j] + outer[1 - j]).astype(BF16)
        for d in range(n):
            c = pltpu.make_async_copy(hidden.at[j], out.at[d, slot, (ny - 1) * half], sems.at[j, d])
            c.start()
            copies.append(c)
    for c in copies:
        c.wait()


def outer_edge(planes):
    half = half_index()
    return (planes.shape[-4] - 1) * half, 2 - 2 * half


def inner_edge(planes):
    half = half_index()
    return (planes.shape[-4] - 1) * (1 - half), 2 * half


def second_edge_kernel(planes, own, other, outer):
    for j, w_ref in enumerate((own, other)):
        for z, v in enumerate(edge(planes, w_ref, *outer_edge(planes))):
            outer[j, z] = v


def channels_first(values):
    return jnp.stack(values, axis=1).astype(BF16)


def ends_role(y, ny):
    return half_index() if y == 0 else 1 - half_index()


def two_parts(v):
    high = v.astype(BF16)
    return high, (v - high.astype(F32)).astype(BF16)


def second_other_kernel(planes, w_ref, bias, v_ref, _, sent, ends):
    ny = planes.shape[-4]
    n = planes.shape[0]
    half = half_index()
    partner = lax.axis_index("ch") + n - 2 * n * half

    def take(_, y, values):
        for z, v in enumerate(values):
            v = v + bias[...]
            whole = v_ref[partner, y + half, z].astype(F32) + v
            if y == 0 or y == ny - 1:
                ends[ends_role(y, ny), z] = whole
            else:
                sent[y - 1, z] = whole.astype(BF16)

    conv(half_cells(planes), ny, planes, (w_ref,), take)
    sent[2], sent[3] = two_parts(ends[1])
    for z, v in enumerate(edge(planes, w_ref, *inner_edge(planes))):
        sent[4, z], sent[5, z] = two_parts(v)


def finish_kernel(ends, outer, sent):
    sent[...] = (ends[0] + outer[0]).astype(BF16)


def second_own_kernel(planes, w_ref, b_ref, v_ref, out, ends, inner_own, mine, sem):
    ny, nz, co, nx = planes.shape[-4:]
    bias = jnp.broadcast_to(column(b_ref, co), (co, nx))
    me, half = lax.axis_index("ch"), half_index()

    def take(_, y, values):
        values = [v_ref[me, y + half, z].astype(F32) + (v + bias) for z, v in enumerate(values)]
        if y == 0 or y == ny - 1:
            for z, v in enumerate(values):
                ends[ends_role(y, ny), z] = v
        else:
            mine[:, y - 1] = channels_first(values)

    conv(half_cells(planes), ny, planes, (w_ref,), take)
    copy = pltpu.make_async_copy(mine, out.at[:, pl.ds(half * ny + 1, ny - 2)], sem)
    copy.start()
    for z, v in enumerate(edge(planes, w_ref, *inner_edge(planes))):
        inner_own[z] = v
    copy.wait()


def outer_end_kernel(ends, outer, _, out, plane, sem):
    ny, half = out.shape[1] // 2, half_index()
    plane[...] = channels_first([ends[0, z] + outer[1, z] for z in range(ends.shape[1])])
    copy = pltpu.make_async_copy(plane, out.at[:, half * ny + (ny - 1) * half], sem)
    copy.start()
    copy.wait()


def last_kernel(ends, inner_own, received, last_plane, _, out, whole, rest, sems):
    nz = ends.shape[1]
    ny, half = out.shape[1] // 2, half_index()
    mine, theirs = half * ny, (1 - half) * ny
    outer, inner = (ny - 1) * half, (ny - 1) * (1 - half)

    def got(at, z):
        return received[at, z].astype(F32)

    ends_at = (
        (mine + inner, lambda z: ends[1, z] + (got(4, z) + got(5, z))),
        (theirs + inner, lambda z: last_plane[z].astype(F32)),
        (theirs + outer, lambda z: (got(2, z) + got(3, z)) + inner_own[z]),
    )
    copies = []
    for i, (at, value) in enumerate(ends_at):
        rest[i] = channels_first([value(z) for z in range(nz)])
        copies.append(pltpu.make_async_copy(rest.at[i], out.at[:, at], sems.at[i]))
        copies[-1].start()
    for y in range(ny - 2):
        whole[:, y] = channels_first([received[y, z].astype(F32) for z in range(nz)])
    copies.append(pltpu.make_async_copy(whole, out.at[:, pl.ds(theirs + 1, ny - 2)], sems.at[3]))
    copies[-1].start()
    for c in copies:
        c.wait()


ANY = pl.BlockSpec(memory_space=pl.ANY)
VMEM = pl.BlockSpec(memory_space=pltpu.VMEM)
DMA = pltpu.SemaphoreType.DMA
PARAMS = pltpu.CompilerParams(vmem_limit_bytes=48 << 20)


LONG = pl.CostEstimate(flops=40_000_000_000, bytes_accessed=1_000_000, transcendentals=0)


def call(kernel, out_shape, in_specs, out_specs, scratch, **extra):
    return pl.pallas_call(
        kernel,
        out_shape=out_shape,
        in_specs=in_specs,
        out_specs=out_specs,
        scratch_shapes=scratch,
        compiler_params=PARAMS,
        name=kernel.__name__,
        **extra,
    )


def three_parts(v):
    parts = []
    for _ in range(3):
        high = lax.reduce_precision(v, 8, 7)
        parts.append(high.astype(BF16))
        v = v - high
    return parts


def per_device(volume, first_weight, first_bias, second_weight, second_bias):
    co, full, nz, nx = volume.shape
    n, length = lax.axis_size("ch"), lax.axis_size("gy")
    g, ny = n // 2, full // 2
    axes = ("gy", "ch")
    f32 = lambda *lead: jax.ShapeDtypeStruct((*lead, nz, co, nx), F32)
    bf16 = lambda *lead: jax.ShapeDtypeStruct((*lead, nz, co, nx), BF16)

    def device(row, half, x):
        return row * n + half * g + x

    def route(*moves):
        return [
            (device(row, half, x), device(row + on, there, x))
            for half, on, there in moves
            for row in range(length)
            if 0 <= row + on < length
            for x in range(g)
        ]

    to_across = route((0, -1, 1), (1, 1, 0))
    to_partner = route((0, 0, 1), (1, 0, 0))
    weights_route = [
        (device(row ^ 2, 1 - half, x), device(row, half, x))
        for row in range(length)
        for half in range(2)
        for x in range(g)
    ]

    core = lax.axis_index("gy") % 2
    taps = 27
    weight = first_weight.reshape(taps, co, -1)
    part = (taps + 1) // 2
    fetched = lax.ppermute(
        lax.dynamic_slice_in_dim(weight, (taps - part) * core, part, axis=0), axes, weights_route
    )
    swapped = lax.ppermute(fetched, "gy", [(i, i ^ 1) for i in range(length)])
    columns = jnp.stack(three_parts(first_bias) + three_parts(second_bias), axis=1)
    slab = jnp.pad(columns, ((0, 0), (0, weight.shape[2] - 6)))
    parcel = jnp.concatenate([second_weight.reshape(weight.shape), slab[None]], axis=0)
    other_second = lax.ppermute(parcel, axes, weights_route)

    cells_first = jnp.transpose(volume, (1, 2, 0, 3))
    sent = call(spread_kernel, bf16(n, ny + 1), [VMEM], ANY, [DMA((n,))])(cells_first)
    main = lax.all_to_all(sent, "ch", 0, 0, tiled=True)

    outer, other_first = call(
        first_edge_kernel,
        (f32(2), jax.ShapeDtypeStruct(weight.shape, BF16)),
        [VMEM] * 4,
        (VMEM,) * 2,
        [],
    )(main, first_weight, fetched, swapped)
    outer = lax.ppermute(outer, axes, to_across)
    hidden, ends, other_bias = call(
        first_kernel,
        (bf16(g, 2, ny), f32(2, 2), jax.ShapeDtypeStruct((co, nx), F32)),
        [VMEM] * 5,
        (ANY, VMEM, VMEM),
        [pltpu.VMEM((2, ny, nz, co, nx), BF16), DMA((2, g))],
    )(main, first_weight, other_first, other_second, first_bias[None])
    hidden = call(
        first_ends_kernel,
        bf16(g, 2, ny),
        [VMEM] * 2 + [ANY],
        ANY,
        [pltpu.VMEM((2, nz, co, nx), BF16), DMA((2, g))],
        input_output_aliases={2: 0},
    )(ends, outer, hidden)

    groups = [list(range(g)), list(range(g, n))]
    gathered = lax.all_to_all(hidden, "ch", 0, 0, tiled=True, axis_index_groups=groups)

    edges = call(second_edge_kernel, f32(2), [VMEM] * 3, VMEM, [])(
        gathered, second_weight, other_second
    )
    outer = lax.ppermute(edges, axes, to_across)
    out_type = jax.ShapeDtypeStruct(volume.shape, BF16)
    sent, ends = call(second_other_kernel, (bf16(6), f32(2)), [VMEM] * 4 + [ANY], (VMEM, VMEM), [])(
        gathered, other_second, other_bias, main, edges
    )
    received = lax.ppermute(sent, axes, to_partner)
    last_plane = call(finish_kernel, bf16(), [VMEM] * 2, VMEM, [], cost_estimate=LONG)(ends, outer)
    last_plane = lax.ppermute(last_plane, axes, to_partner)
    out, ends, inner_own = call(
        second_own_kernel,
        (out_type, f32(2), f32()),
        [VMEM] * 4,
        (ANY, VMEM, VMEM),
        [pltpu.VMEM((co, ny - 2, nz, nx), BF16), DMA],
    )(gathered, second_weight, second_bias[None], main)
    out = call(
        outer_end_kernel,
        out_type,
        [VMEM, VMEM, ANY],
        ANY,
        [pltpu.VMEM((co, nz, nx), BF16), DMA],
        input_output_aliases={2: 0},
    )(ends, outer, out)
    return call(
        last_kernel,
        out_type,
        [VMEM] * 4 + [ANY],
        ANY,
        [pltpu.VMEM((co, ny - 2, nz, nx), BF16), pltpu.VMEM((3, co, nz, nx), BF16), DMA((4,))],
        input_output_aliases={4: 0},
    )(ends, inner_own, received, last_plane, out)


def solution(mesh):
    in_specs = (
        P("ch", "gy", None, None),
        P(None, None, None, "ch", None),
        P("ch"),
        P(None, None, None, "ch", None),
        P("ch"),
    )
    out_specs = P("ch", "gy", None, None)
    return jax.shard_map(
        per_device, mesh=mesh, in_specs=in_specs, out_specs=out_specs, check_vma=False
    )
```
